32 devices in a mesh: dp: 2 (over x), tok: 16 (over z, y, core).
Axes of the slice: x: 2, y: 2, z: 4, core: 2. Of those that a mesh axis runs over, the one named last changes fastest.
Arguments:
- row_input: bfloat16 [16, 1024, 1024], P('tok', None, 'dp'), may hold values from -6 to 6
- out_grad: bfloat16 [16, 1024, 1024], P('tok', None, 'dp'), may hold values from -6 to 6
- in_weight: bfloat16 [2, 16, 1024, 1024], P(None, 'tok'), may hold values from -0.1875 to 0.1875
- out_weight: bfloat16 [2, 16, 1024, 1024], P(None, 'tok'), may hold values from -0.1875 to 0.1875
Outputs:
- grad_rows: bfloat16 [16, 1024, 1024], P('tok', None, 'dp')
- grad_in_weight: bfloat16 [2, 16, 1024, 1024], P(None, 'tok', 'dp')
- grad_out_weight: bfloat16 [2, 16, 1024, 1024], P(None, 'tok', None, 'dp')
The draws below stay inside these ranges and needn't reach their ends.
All inputs are finite; a program needn't handle non-finite values.
Results may differ from the reference program's by a relative error of at most 0.015.
Values may be sent and summed in bfloat16 or wider, within the bound.
A program may use at most 128 MiB of HBM per device.

```python
import jax
import jax.numpy as jnp
from jax import lax

D = 1024
H = 1024
T_SIZE = 16
ROWS_DEV = 512
ROWS = 1024
BLOCKS = 2
N_DP = 2


def block_levels(key, dims, pieces, low, high):
    loudness = 1.0
    for dim, blocks in pieces:
        steps = jax.random.uniform(jax.random.fold_in(jax.random.fold_in(key, 6), dim), (blocks,), jnp.float32, low / len(pieces), high / len(pieces))
        loudness = loudness * jnp.repeat(jnp.exp(steps), dims[dim] // blocks).reshape((-1,) + (1,) * (len(dims) - 1 - dim))
    return loudness


def bell_draw(key, shape, width, limit, shards=(), held_as=jnp.bfloat16):
    gain = block_levels(key, shape, shards, -0.22, 0.18) if shards else 1.0
    result = jax.random.normal(key, shape, jnp.float32) * width * gain
    return jnp.minimum(jnp.maximum(result, -limit), limit).astype(held_as)


def setup_inputs(seed: int = 0) -> dict:
    seeds = jax.random.split(jax.random.key(seed), 5)
    return {
        "row_input": bell_draw(seeds[0], (T_SIZE, D, ROWS), 1.0, 6.0, ((0, 16), (2, 2))),
        "out_grad": bell_draw(seeds[1], (T_SIZE, D, ROWS), 1.0, 6.0, ((0, 16), (2, 2))),
        "in_weight": bell_draw(seeds[2], (BLOCKS, T_SIZE, D, H), D ** -0.5, 0.1875, ((1, 16),)),
        "out_weight": bell_draw(seeds[3], (BLOCKS, T_SIZE, H, D), H ** -0.5, 0.1875, ((1, 16),)),
    }


epsilon = 1e-05

def mixing(values):
    token_count, feature_width, row_count = values.shape
    head_size = feature_width // token_count
    grouped = values.reshape(token_count, token_count, head_size, row_count)
    return grouped.transpose(1, 0, 2, 3).reshape(token_count, feature_width, row_count)

def normalize(values):
    center = values - lax.optimization_barrier(jnp.mean(values, axis=1, keepdims=True))
    inverse = lax.rsqrt(lax.optimization_barrier(jnp.mean(center * center, axis=1, keepdims=True)) + epsilon)
    return (center * inverse, inverse)

def norm_back(normal, inverse, upward):
    mean_up = lax.optimization_barrier(jnp.mean(upward, axis=1, keepdims=True))
    mean_cross = lax.optimization_barrier(jnp.mean(upward * normal, axis=1, keepdims=True))
    return inverse * (upward - mean_up - normal * mean_cross)

def gelu_parts(hidden):
    cumulative = 0.5 * (1.0 + lax.erf(hidden * 0.7071067811865476))
    density = jnp.exp(-0.5 * hidden * hidden) * 0.3989422804014327
    return (hidden * cumulative, cumulative + hidden * density)

def row_block_sum(left_side, right_side, form):
    total_sum = None
    for number in range(N_DP):
        offset = number * ROWS_DEV
        left_rows = left_side[:, :, offset:offset + ROWS_DEV].astype(jnp.float32)
        right_rows = right_side[:, :, offset:offset + ROWS_DEV].astype(jnp.float32)
        term_sum = jnp.einsum(form, left_rows, right_rows)
        rounded = lax.optimization_barrier(term_sum.astype(jnp.bfloat16)).astype(jnp.float32)
        total_sum = rounded if total_sum is None else total_sum + rounded
    return total_sum.astype(jnp.bfloat16)

def reference(row_input, out_grad, in_weight, out_weight):
    caches = []
    current = row_input
    for number in range(BLOCKS):
        weight_first = in_weight[number].astype(jnp.float32)
        weight_second = out_weight[number].astype(jnp.float32)
        mixture = mixing(current)
        summed = mixture.astype(jnp.float32) + current.astype(jnp.float32)
        summed_hat, summed_inv = normalize(summed)
        normed = summed_hat.astype(jnp.bfloat16)
        hidden = jnp.einsum('tdh,tdr->thr', weight_first, normed.astype(jnp.float32))
        active_full, derivative = gelu_parts(hidden)
        active = active_full.astype(jnp.bfloat16)
        second = jnp.einsum('thd,thr->tdr', weight_second, active.astype(jnp.float32)) + normed.astype(jnp.float32)
        second_hat, second_inv = normalize(second)
        caches.append((summed_hat, summed_inv, normed, derivative, active, second_hat, second_inv))
        current = second_hat.astype(jnp.bfloat16)
    upward = out_grad
    grads_first = [None] * BLOCKS
    grads_second = [None] * BLOCKS
    for number in reversed(range(BLOCKS)):
        summed_hat, summed_inv, normed, derivative, active, second_hat, second_inv = caches[number]
        weight_first = in_weight[number].astype(jnp.float32)
        weight_second = out_weight[number].astype(jnp.float32)
        dsecond = norm_back(second_hat, second_inv, upward.astype(jnp.float32))
        dsecond_low = dsecond.astype(jnp.bfloat16)
        dhidden = (jnp.einsum('thd,tdr->thr', weight_second, dsecond_low.astype(jnp.float32)) * derivative).astype(jnp.bfloat16)
        inner = jnp.einsum('tdh,thr->tdr', weight_first, dhidden.astype(jnp.float32)) + dsecond
        dsummed = norm_back(summed_hat, summed_inv, inner)
        dsummed_low = dsummed.astype(jnp.bfloat16)
        upward = (dsummed + mixing(dsummed_low).astype(jnp.float32)).astype(jnp.bfloat16)
        grads_second[number] = row_block_sum(active, dsecond_low, 'thr,tdr->thd')
        grads_first[number] = row_block_sum(normed, dhidden, 'tdr,thr->tdh')
    return (upward, jnp.stack(grads_first), jnp.stack(grads_second))
```

```python
import functools

import jax
import jax.numpy as jnp
from jax import lax
from jax.experimental import pallas as pl
from jax.experimental.pallas import tpu as pltpu
from jax.sharding import PartitionSpec as P

epsilon = 1e-05
MESH = pl.DeviceIdType.MESH
F32 = jnp.float32
BF16 = jnp.bfloat16


def gelu_parts(hidden):
    cumulative = 0.5 * (1.0 + lax.erf(hidden * 0.7071067811865476))
    density = jnp.exp(-0.5 * hidden * hidden) * 0.3989422804014327
    return (hidden * cumulative, cumulative + hidden * density)


def kernel(
    n_tok, n_dp, cuts, tile, span, piece,
    x_hbm, g_hbm, wi_hbm, wo_hbm,
    orow, gi_s, go_s,
    x_in, x_hat, recv, grad, wi, wo, wit, wot, normed, act, deriv, dsl, dhid, low, dsum,
    normed_p, dsl_p, deriv_p, dhid_p, tmp, inv1, inv2, inv_p,
    ld_sem, z_send, z_recv, x_send, x_recv, p_send, p_recv,
):
    blocks, width, hid = wi.shape
    rows = x_in.shape[2]
    head = width // n_tok
    half = width // n_dp
    me = lax.axis_index("tok")
    mine = lax.axis_index("dp")
    other = lax.rem(mine + 1, n_dp)

    loads = []
    for c in range(cuts):
        loads.append(pltpu.make_async_copy(x_hbm.at[0, :, pl.ds(c * rows, rows)], x_in.at[c], ld_sem.at[c]))
    for c in range(cuts):
        loads.append(pltpu.make_async_copy(g_hbm.at[0, :, pl.ds(c * rows, rows)], grad.at[c], ld_sem.at[cuts + c]))
    for k in range(blocks):
        loads.append(pltpu.make_async_copy(wi_hbm.at[k, 0], wi.at[k], ld_sem.at[2 * cuts + 2 * k]))
        loads.append(pltpu.make_async_copy(wo_hbm.at[k, 0], wo.at[k], ld_sem.at[2 * cuts + 2 * k + 1]))
    for load in loads:
        load.start()

    barrier = pltpu.get_barrier_semaphore()

    def greet(i, carry):
        peer = lax.rem(me + 1 + i, n_tok)
        pl.semaphore_signal(barrier, inc=1, device_id={"tok": peer}, device_id_type=MESH)
        return carry

    lax.fori_loop(0, n_tok - 1, greet, 0)
    pl.semaphore_signal(barrier, inc=1, device_id={"dp": other}, device_id_type=MESH)
    pl.semaphore_wait(barrier, n_tok)

    def mix_send(src, m, c):
        def one(i, carry):
            step = 1 + lax.rem(i + n_tok // 2 - 1, n_tok - 1)
            peer = lax.rem(me + step, n_tok)
            pltpu.make_async_remote_copy(
                src_ref=src.at[pl.ds(pl.multiple_of(peer * head, head), head)],
                dst_ref=recv.at[m, c, pl.ds(pl.multiple_of(me * head, head), head)],
                send_sem=z_send.at[m, c],
                recv_sem=z_recv.at[m, c],
                device_id={"tok": peer},
                device_id_type=MESH,
            ).start()
            return carry

        lax.fori_loop(0, n_tok - 1, one, 0)
        own = pl.ds(pl.multiple_of(me * head, head), head)
        recv[m, c, own, :] = src[own, :]

    def mix_all(m, c):
        part = recv.at[m, c, pl.ds(0, head * (n_tok - 1))]
        return pltpu.make_async_remote_copy(
            src_ref=part, dst_ref=part, send_sem=z_send.at[m, c], recv_sem=z_recv.at[m, c],
            device_id={"tok": lax.rem(me + 1, n_tok)}, device_id_type=MESH,
        )

    team = n_tok // 2
    base = (me // team) * team
    far = pl.ds(pl.multiple_of((team - base) * head, head), team * head)

    def team_send(k, c):
        def one(i, carry):
            peer = base + lax.rem(me - base + 1 + i, team)
            pltpu.make_async_remote_copy(
                src_ref=dhid_p.at[c, pl.ds(pl.multiple_of(peer * head, head), head)],
                dst_ref=normed_p.at[k, c, pl.ds(pl.multiple_of(me * head, head), head)],
                send_sem=p_send.at[k, c],
                recv_sem=p_recv.at[k, c],
                device_id={"tok": peer},
                device_id_type=MESH,
            ).start()
            return carry

        lax.fori_loop(0, team - 1, one, 0)
        own = pl.ds(pl.multiple_of(me * head, head), head)
        normed_p[k, c, own, :] = dhid_p[c, own, :]

    def team_all(k, c):
        part = normed_p.at[k, c, pl.ds(0, head * (team - 1))]
        return pltpu.make_async_remote_copy(
            src_ref=part, dst_ref=part, send_sem=p_send.at[k, c], recv_sem=p_recv.at[k, c],
            device_id={"tok": lax.rem(me + 1, n_tok)}, device_id_type=MESH,
        )

    def pair_part(kind, k, c, at):
        if kind == 0:
            src, dst = normed.at[k, c], normed_p.at[k, c]
        elif kind == 2:
            src, dst = recv.at[k, c], normed_p.at[k, c]
        else:
            src, dst = grad.at[c] if k == blocks - 1 else dsl.at[k, c], dsl_p.at[k, c]
        return pltpu.make_async_remote_copy(
            src_ref=src.at[at], dst_ref=dst.at[at],
            send_sem=x_send.at[kind, k, c], recv_sem=x_recv.at[kind, k, c],
            device_id={"dp": other}, device_id_type=MESH,
        )

    def pair(kind, k, c):
        return pair_part(kind, k, c, far if kind == 2 else pl.ds(0, width))

    def pair_send(kind, k, c):
        def one(i, carry):
            pair_part(kind, k, c, pl.ds(pl.multiple_of(i * piece, piece), piece)).start()
            return carry

        lax.fori_loop(0, width // piece, one, 0)

    def tiles(body, carry=0):
        def step(i, state):
            return body(pl.ds(pl.multiple_of(i * tile, tile), tile), state)

        return lax.fori_loop(0, width // tile, step, carry)

    zero = jnp.zeros((8, rows), F32)

    def fold(value):
        return jnp.sum(value.reshape(tile // 8, 8, rows), axis=0)

    def mean(total):
        return jnp.sum(total, axis=0, keepdims=True) * (1.0 / width)

    stride = min(2 * span, width)

    def matmul(left, right, sink):
        def step(i, carry):
            at = pl.ds(pl.multiple_of(i * stride, stride), stride)
            sink(at, jnp.dot(left[at, :], right[...], preferred_element_type=F32))
            return carry

        lax.fori_loop(0, left.shape[0] // stride, step, 0)

    def to_tmp(at, value):
        tmp[at, :] = value

    def norm_tmp(total, inv_ref, out_ref):
        center = mean(total)

        def spread(at, state):
            gap = tmp[at, :] - center
            return state + fold(gap * gap)

        inverse = lax.rsqrt(mean(tiles(spread, zero)) + epsilon)
        inv_ref[...] = inverse

        def write(at, state):
            out_ref[at, :] = ((tmp[at, :] - center) * inverse).astype(BF16)
            return state

        tiles(write)

    def forward(k, c):
        current = x_in.at[c] if k == 0 else x_hat.at[k - 1, c]

        def add(at, state):
            value = recv[k, c, at, :].astype(F32) + current[at, :].astype(F32)
            tmp[at, :] = value
            return state + fold(value)

        norm_tmp(tiles(add, zero), inv1.at[k, c], normed.at[k, c])
        if k == 0:
            pair_send(0, k, c)
        matmul(wit.at[k], normed.at[k, c], to_tmp)

        def gelu(at, state):
            first, second = gelu_parts(tmp[at, :])
            act[k, c, at, :] = first.astype(BF16)
            deriv[k, c, at, :] = second
            return state

        tiles(gelu)
        matmul(wot.at[k], act.at[k, c], to_tmp)

        def skip(at, state):
            value = tmp[at, :] + normed[k, c, at, :].astype(F32)
            tmp[at, :] = value
            return state + fold(value)

        norm_tmp(tiles(skip, zero), inv2.at[k, c], x_hat.at[k, c])

    def norm_back(means, hat, inverse, sink):
        up, cross = mean(means[0]), mean(means[1])

        def write(at, state):
            value = inverse * (tmp[at, :] - up - hat[at, :].astype(F32) * cross)
            sink(at, value)
            return state

        tiles(write)

    def backward(k, c):
        def upward(at, state):
            if k == blocks - 1:
                value = grad[c, at, :].astype(F32)
            else:
                value = dsum[c, at, :] + recv[2 * blocks - 2 - k, c, at, :].astype(F32)
                value = value.astype(BF16).astype(F32)
            tmp[at, :] = value
            return state[0] + fold(value), state[1] + fold(value * x_hat[k, c, at, :].astype(F32))

        def keep_second(at, value):
            tmp[at, :] = value
            dsl[k, c, at, :] = value.astype(BF16)

        norm_back(tiles(upward, (zero, zero)), x_hat.at[k, c], inv2[k, c], keep_second)
        if k < blocks - 1:
            pair_send(1, k, c)

        def hidden_sink(at, value):
            dhid[k, c, at, :] = (value * deriv[k, c, at, :]).astype(BF16)

        matmul(wo.at[k], dsl.at[k, c], hidden_sink)

        def add_tmp(at, value):
            tmp[at, :] = tmp[at, :] + value

        matmul(wi.at[k], dhid.at[k, c], add_tmp)

        def sums(at, state):
            value = tmp[at, :]
            return state[0] + fold(value), state[1] + fold(value * normed[k, c, at, :].astype(F32))

        def keep_summed(at, value):
            dsum[c, at, :] = value
            low[k, c, at, :] = value.astype(BF16)

        norm_back(tiles(sums, (zero, zero)), normed.at[k, c], inv1[k, c], keep_summed)
        mix_send(low.at[k, c], 2 * blocks - 1 - k, c)

    def peer_forward(k, c):
        if k == 0:
            pair(0, k, c).wait_recv()
        else:
            team_all(k, c).wait()
            pair(2, k, c).wait()

            def add(at, state):
                value = normed_p[k, c, at, :].astype(F32) + dhid_p[c, at, :].astype(F32)
                tmp[at, :] = value
                return state + fold(value)

            norm_tmp(tiles(add, zero), inv_p, normed_p.at[k, c])
        matmul(wit.at[k], normed_p.at[k, c], to_tmp)

        def gelu(at, state):
            first, second = gelu_parts(tmp[at, :])
            recv[k, c, at, :] = first.astype(BF16)
            deriv_p[k, c, at, :] = second.astype(BF16)
            return state

        tiles(gelu)
        matmul(wot.at[k], recv.at[k, c], to_tmp)

        def skip(at, state):
            value = tmp[at, :] + normed_p[k, c, at, :].astype(F32)
            tmp[at, :] = value
            return state + fold(value)

        norm_tmp(tiles(skip, zero), inv_p, dhid_p.at[c])
        if k < blocks - 1:
            team_send(k + 1, c)
            return
        pair(1, k, c).wait_recv()

        def upward(at, state):
            value = dsl_p[k, c, at, :].astype(F32)
            tmp[at, :] = value
            return state[0] + fold(value), state[1] + fold(value * dhid_p[c, at, :].astype(F32))

        def keep(at, value):
            dsl_p[k, c, at, :] = value.astype(BF16)

        norm_back(tiles(upward, (zero, zero)), dhid_p.at[c], inv_p[...], keep)

    def peer_backward(k, c):
        if k < blocks - 1:
            pair(1, k, c).wait_recv()

        def sink(at, value):
            dhid_p[c, at, :] = (value * deriv_p[k, c, at, :].astype(F32)).astype(BF16)

        matmul(wo.at[k], dsl_p.at[k, c], sink)

    def outer(left, right):
        return lax.dot_general(left, right, (((1,), (1,)), ((), ())), preferred_element_type=F32)

    part = pl.ds(pl.multiple_of(mine * half, half), half)

    def bands(size, body):
        def step(i, carry):
            body(i * span)
            return carry

        lax.fori_loop(0, size // span, step, 0)

    def band(start):
        return pl.ds(pl.multiple_of(start, span), span)

    def own_grads(k):
        def first(start):
            src = band(mine * half + start)
            total = sum(outer(normed[k, c, src, :], dhid[k, c]) for c in range(cuts))
            gi_s[k, 0, band(start), :] = total.astype(BF16)

        bands(half, first)

        def second(start):
            at = band(start)
            total = sum(outer(act[k, c, at, :], dsl[k, c, part, :]) for c in range(cuts))
            go_s[k, 0, at, :] = total.astype(BF16)

        bands(hid, second)

    def peer_grads(k):
        def put(out, at, total):
            out[k, 0, at, :] = (out[k, 0, at, :].astype(F32) + total.astype(BF16).astype(F32)).astype(BF16)

        def first(start):
            src = band(mine * half + start)
            put(gi_s, band(start), sum(outer(normed_p[k, c, src, :], dhid_p[c]) for c in range(cuts)))

        bands(half, first)

        def second(start):
            at = band(start)
            put(go_s, at, sum(outer(recv[k, c, at, :], dsl_p[k, c, part, :]) for c in range(cuts)))

        bands(hid, second)

    def each(body):
        def step(c, carry):
            body(c)
            return carry

        lax.fori_loop(0, cuts, step, 0)

    for c in range(cuts):
        loads[c].wait()
        mix_send(x_in.at[c], 0, c)
    for c in range(cuts):
        loads[cuts + c].wait()
    pair_send(1, blocks - 1, 0)
    for load in loads[2 * cuts:]:
        load.wait()
    edge = min(256, width, hid)

    def flip(i, carry):
        a = pl.ds(pl.multiple_of(lax.rem(i, hid // edge) * edge, edge), edge)
        for k in range(blocks):
            for j in range(width // edge):
                b = pl.ds(j * edge, edge)
                wit[k, a, b] = wi[k, b, a].T
                wot[k, b, a] = wo[k, a, b].T
        return carry

    lax.fori_loop(0, hid // edge, flip, 0)

    def ahead(k, c):
        if k > 0:
            peer_forward(k - 1, c)
        mix_all(k, c).wait_recv()
        if k > 0:
            pair_part(2, k, c, far).start()
        forward(k, c)
        if k < blocks - 1:
            mix_send(x_hat.at[k, c], k + 1, c)
        else:
            backward(k, c)

    def last_ahead(c):
        peer_forward(blocks - 1, c)
        peer_backward(blocks - 1, c)
        mix_all(blocks, c).wait_recv()
        backward(blocks - 2, c)

    def finish(c):
        mix_all(2 * blocks - 1, c).wait_recv()

        def write(at, state):
            orow[0, at, pl.ds(c * rows, rows)] = (dsum[c, at, :] + recv[2 * blocks - 1, c, at, :].astype(F32)).astype(BF16)
            return state

        tiles(write)

    each(functools.partial(ahead, 0))
    for c in range(1, cuts):
        pair_send(1, blocks - 1, c)
    for k in range(1, blocks):
        each(functools.partial(ahead, k))
    own_grads(blocks - 1)
    each(last_ahead)
    peer_grads(blocks - 1)
    for k in reversed(range(blocks - 1)):
        own_grads(k)
        each(functools.partial(peer_backward, k))
        peer_grads(k)
    for c in range(cuts):
        finish(c)
    for c in range(cuts):
        pair(0, 0, c).wait_send()
        for k in range(blocks):
            pair(1, k, c).wait_send()
        for m in range(2 * blocks):
            mix_all(m, c).wait_send()


def store(count, *refs):
    sem = refs[-1]
    moves = []
    for src, dst in zip(refs[:count], refs[count:2 * count]):
        for k in range(src.shape[0]):
            for r in range(4):
                step = src.shape[-2] // 4
                at = (k,) + (0,) * (len(src.shape) - 3) + (pl.ds(r * step, step),)
                moves.append(pltpu.make_async_copy(src.at[at], dst.at[at], sem.at[len(moves)]))
    for move in moves:
        move.start()
    for move in moves:
        move.wait()


def written(values):
    count = len(values)
    pieces = sum(4 * v.shape[0] for v in values)
    return pl.pallas_call(
        functools.partial(store, count),
        out_shape=tuple(jax.ShapeDtypeStruct(v.shape, v.dtype) for v in values),
        in_specs=[pl.BlockSpec(memory_space=pltpu.VMEM)] * count,
        out_specs=[pl.BlockSpec(memory_space=pl.ANY)] * count,
        scratch_shapes=[pltpu.SemaphoreType.DMA((pieces,))],
        compiler_params=pltpu.CompilerParams(vmem_limit_bytes=1024 * 1024),
    )(*values)


def per_device(n_tok, n_dp, row_input, out_grad, in_weight, out_weight):
    blocks, _, width, hid = in_weight.shape
    row_count = row_input.shape[2]
    cuts = max(1, row_count // 256)
    rows = row_count // cuts
    half = width // n_dp
    wide = (cuts, width, rows)
    deep = (cuts, hid, rows)
    vm = pltpu.VMEM
    dma = pltpu.SemaphoreType.DMA
    return written(pl.pallas_call(
        functools.partial(kernel, n_tok, n_dp, cuts, 64, 256, width),
        out_shape=(
            pltpu.VMEM(row_input.shape, BF16),
            pltpu.VMEM((blocks, 1, half, hid), BF16),
            pltpu.VMEM((blocks, 1, hid, half), BF16),
        ),
        in_specs=[pl.BlockSpec(memory_space=pl.ANY)] * 4,
        out_specs=[pl.BlockSpec(memory_space=pltpu.VMEM)] * 3,
        scratch_shapes=[
            vm(wide, BF16),
            vm((blocks,) + wide, BF16),
            vm((2 * blocks,) + wide, BF16),
            vm(wide, BF16),
            vm((blocks, width, hid), BF16),
            vm((blocks, hid, width), BF16),
            vm((blocks, hid, width), BF16),
            vm((blocks, width, hid), BF16),
            vm((blocks,) + wide, BF16),
            vm((blocks,) + deep, BF16),
            vm((blocks,) + deep, F32),
            vm((blocks,) + wide, BF16),
            vm((blocks,) + deep, BF16),
            vm((blocks,) + wide, BF16),
            vm(wide, F32),
            vm((blocks,) + wide, BF16),
            vm((blocks,) + wide, BF16),
            vm((blocks,) + deep, BF16),
            vm(deep, BF16),
            vm((width, rows), F32),
            vm((blocks, cuts, 1, rows), F32),
            vm((blocks, cuts, 1, rows), F32),
            vm((1, rows), F32),
            dma((2 * cuts + 2 * blocks,)),
            dma((2 * blocks, cuts)),
            dma((2 * blocks, cuts)),
            dma((3, blocks, cuts)),
            dma((3, blocks, cuts)),
            dma((blocks, cuts)),
            dma((blocks, cuts)),
        ],
        compiler_params=pltpu.CompilerParams(
            collective_id=0, has_side_effects=True, vmem_limit_bytes=57 * 1024 * 1024
        ),
    )(row_input, out_grad, in_weight, out_weight))


def solution(mesh):
    return jax.shard_map(
        functools.partial(per_device, mesh.shape["tok"], mesh.shape["dp"]),
        mesh=mesh,
        in_specs=(
            P("tok", None, "dp"),
            P("tok", None, "dp"),
            P(None, "tok", None, None),
            P(None, "tok", None, None),
        ),
        out_specs=(P("tok", None, "dp"), P(None, "tok", "dp", None), P(None, "tok", None, "dp")),
        check_vma=False,
    )
```

```python
import functools

import jax
import jax.numpy as jnp
from jax import lax
from jax.experimental import pallas as pl
from jax.experimental.pallas import tpu as pltpu
from jax.sharding import PartitionSpec as P

epsilon = 1e-05
MESH = pl.DeviceIdType.MESH
F32 = jnp.float32
BF16 = jnp.bfloat16


def gelu_parts(hidden):
    cumulative = 0.5 * (1.0 + lax.erf(hidden * 0.7071067811865476))
    density = jnp.exp(-0.5 * hidden * hidden) * 0.3989422804014327
    return (hidden * cumulative, cumulative + hidden * density)


def kernel(
    n_tok, n_dp, cuts, tile, span, piece,
    x_hbm, g_hbm, wi_hbm, wo_hbm,
    orow, gi_s, go_s,
    x_in, x_hat, recv, grad, wi, wo, wit, wot, normed, act, deriv, dsl, dhid, low, dsum,
    normed_p, dsl_p, deriv_p, dhid_p, tmp, inv1, inv2, inv_p,
    ld_sem, z_send, z_recv, x_send, x_recv, p_send, p_recv,
):
    blocks, width, hid = wi.shape
    rows = x_in.shape[2]
    head = width // n_tok
    half = width // n_dp
    me = lax.axis_index("tok")
    mine = lax.axis_index("dp")
    other = lax.rem(mine + 1, n_dp)

    loads = []
    for c in range(cuts):
        loads.append(pltpu.make_async_copy(x_hbm.at[0, :, pl.ds(c * rows, rows)], x_in.at[c], ld_sem.at[c]))
    for c in range(cuts):
        loads.append(pltpu.make_async_copy(g_hbm.at[0, :, pl.ds(c * rows, rows)], grad.at[c], ld_sem.at[cuts + c]))
    for k in range(blocks):
        loads.append(pltpu.make_async_copy(wi_hbm.at[k, 0], wi.at[k], ld_sem.at[2 * cuts + 2 * k]))
        loads.append(pltpu.make_async_copy(wo_hbm.at[k, 0], wo.at[k], ld_sem.at[2 * cuts + 2 * k + 1]))
    for load in loads:
        load.start()

    barrier = pltpu.get_barrier_semaphore()

    def greet(i, carry):
        peer = lax.rem(me + 1 + i, n_tok)
        pl.semaphore_signal(barrier, inc=1, device_id={"tok": peer}, device_id_type=MESH)
        return carry

    lax.fori_loop(0, n_tok - 1, greet, 0)
    pl.semaphore_signal(barrier, inc=1, device_id={"dp": other}, device_id_type=MESH)
    pl.semaphore_wait(barrier, n_tok)

    team = n_tok // 2
    base = (me // team) * team
    lower = base == 0
    outer_half = jnp.where(lower, me, n_tok - 1 - me) < team // 2

    def spot(i):
        if team % 4:
            return i
        return i - lax.rem(i, 4) + 2 * lax.rem(i, 2) + lax.div(lax.rem(i, 4), 2)

    def mix_send(src, m, c):
        def go(peer):
            pltpu.make_async_remote_copy(
                src_ref=src.at[pl.ds(pl.multiple_of(peer * head, head), head)],
                dst_ref=recv.at[m, c, pl.ds(pl.multiple_of(me * head, head), head)],
                send_sem=z_send.at[m, c],
                recv_sem=z_recv.at[m, c],
                device_id={"tok": peer},
                device_id_type=MESH,
            ).start()

        def cross(i, carry):
            at = spot(i)
            go(jnp.where(lower, n_tok - 1 - at, at))
            return carry

        def local(i, carry):
            at = spot(lax.rem(i + team // 2, team))
            peer = jnp.where(lower, at, n_tok - 1 - at)
            pl.when(peer != me)(functools.partial(go, peer))
            return carry

        @pl.when(outer_half)
        def _():
            lax.fori_loop(0, team, lambda i, carry: local(i, cross(i, carry)), 0)

        @pl.when(jnp.logical_not(outer_half))
        def _():
            lax.fori_loop(0, team, cross, 0)
            lax.fori_loop(0, team, local, 0)

        own = pl.ds(pl.multiple_of(me * head, head), head)
        recv[m, c, own, :] = src[own, :]

    def mix_all(m, c):
        part = recv.at[m, c, pl.ds(0, head * (n_tok - 1))]
        return pltpu.make_async_remote_copy(
            src_ref=part, dst_ref=part, send_sem=z_send.at[m, c], recv_sem=z_recv.at[m, c],
            device_id={"tok": lax.rem(me + 1, n_tok)}, device_id_type=MESH,
        )

    far = pl.ds(pl.multiple_of((team - base) * head, head), team * head)

    def team_send(k, c):
        def one(i, carry):
            peer = base + lax.rem(me - base + 1 + i, team)
            pltpu.make_async_remote_copy(
                src_ref=dhid_p.at[c, pl.ds(pl.multiple_of(peer * head, head), head)],
                dst_ref=normed_p.at[k, c, pl.ds(pl.multiple_of(me * head, head), head)],
                send_sem=p_send.at[k, c],
                recv_sem=p_recv.at[k, c],
                device_id={"tok": peer},
                device_id_type=MESH,
            ).start()
            return carry

        lax.fori_loop(0, team - 1, one, 0)
        own = pl.ds(pl.multiple_of(me * head, head), head)
        normed_p[k, c, own, :] = dhid_p[c, own, :]

    def team_all(k, c):
        part = normed_p.at[k, c, pl.ds(0, head * (team - 1))]
        return pltpu.make_async_remote_copy(
            src_ref=part, dst_ref=part, send_sem=p_send.at[k, c], recv_sem=p_recv.at[k, c],
            device_id={"tok": lax.rem(me + 1, n_tok)}, device_id_type=MESH,
        )

    def pair_part(kind, k, c, at):
        if kind == 0:
            src, dst = normed.at[k, c], normed_p.at[k, c]
        elif kind == 2:
            src, dst = recv.at[k, c], normed_p.at[k, c]
        else:
            src, dst = grad.at[c] if k == blocks - 1 else dsl.at[k, c], dsl_p.at[k, c]
        return pltpu.make_async_remote_copy(
            src_ref=src.at[at], dst_ref=dst.at[at],
            send_sem=x_send.at[kind, k, c], recv_sem=x_recv.at[kind, k, c],
            device_id={"dp": other}, device_id_type=MESH,
        )

    def pair(kind, k, c):
        return pair_part(kind, k, c, far if kind == 2 else pl.ds(0, width))

    def pair_send(kind, k, c):
        def one(i, carry):
            pair_part(kind, k, c, pl.ds(pl.multiple_of(i * piece, piece), piece)).start()
            return carry

        lax.fori_loop(0, width // piece, one, 0)

    def tiles(body, carry=0):
        def step(i, state):
            return body(pl.ds(pl.multiple_of(i * tile, tile), tile), state)

        return lax.fori_loop(0, width // tile, step, carry)

    zero = jnp.zeros((8, rows), F32)

    def fold(value):
        return jnp.sum(value.reshape(tile // 8, 8, rows), axis=0)

    def mean(total):
        return jnp.sum(total, axis=0, keepdims=True) * (1.0 / width)

    stride = min(2 * span, width)

    def matmul(left, right, sink):
        def step(i, carry):
            at = pl.ds(pl.multiple_of(i * stride, stride), stride)
            sink(at, jnp.dot(left[at, :], right[...], preferred_element_type=F32))
            return carry

        lax.fori_loop(0, left.shape[0] // stride, step, 0)

    def to_tmp(at, value):
        tmp[at, :] = value

    def norm_tmp(total, inv_ref, out_ref):
        center = mean(total)

        def spread(at, state):
            gap = tmp[at, :] - center
            return state + fold(gap * gap)

        inverse = lax.rsqrt(mean(tiles(spread, zero)) + epsilon)
        inv_ref[...] = inverse

        def write(at, state):
            out_ref[at, :] = ((tmp[at, :] - center) * inverse).astype(BF16)
            return state

        tiles(write)

    def forward(k, c):
        current = x_in.at[c] if k == 0 else x_hat.at[k - 1, c]

        def add(at, state):
            value = recv[k, c, at, :].astype(F32) + current[at, :].astype(F32)
            tmp[at, :] = value
            return state + fold(value)

        norm_tmp(tiles(add, zero), inv1.at[k, c], normed.at[k, c])
        if k == 0:
            pair_send(0, k, c)
        matmul(wit.at[k], normed.at[k, c], to_tmp)

        def gelu(at, state):
            first, second = gelu_parts(tmp[at, :])
            act[k, c, at, :] = first.astype(BF16)
            deriv[k, c, at, :] = second
            return state

        tiles(gelu)
        matmul(wot.at[k], act.at[k, c], to_tmp)

        def skip(at, state):
            value = tmp[at, :] + normed[k, c, at, :].astype(F32)
            tmp[at, :] = value
            return state + fold(value)

        norm_tmp(tiles(skip, zero), inv2.at[k, c], x_hat.at[k, c])

    def norm_back(means, hat, inverse, sink):
        up, cross = mean(means[0]), mean(means[1])

        def write(at, state):
            value = inverse * (tmp[at, :] - up - hat[at, :].astype(F32) * cross)
            sink(at, value)
            return state

        tiles(write)

    def backward(k, c):
        def upward(at, state):
            if k == blocks - 1:
                value = grad[c, at, :].astype(F32)
            else:
                value = dsum[c, at, :] + recv[2 * blocks - 2 - k, c, at, :].astype(F32)
                value = value.astype(BF16).astype(F32)
            tmp[at, :] = value
            return state[0] + fold(value), state[1] + fold(value * x_hat[k, c, at, :].astype(F32))

        def keep_second(at, value):
            tmp[at, :] = value
            dsl[k, c, at, :] = value.astype(BF16)

        norm_back(tiles(upward, (zero, zero)), x_hat.at[k, c], inv2[k, c], keep_second)
        if k < blocks - 1:
            pair_send(1, k, c)

        def hidden_sink(at, value):
            dhid[k, c, at, :] = (value * deriv[k, c, at, :]).astype(BF16)

        matmul(wo.at[k], dsl.at[k, c], hidden_sink)

        def add_tmp(at, value):
            tmp[at, :] = tmp[at, :] + value

        matmul(wi.at[k], dhid.at[k, c], add_tmp)

        def sums(at, state):
            value = tmp[at, :]
            return state[0] + fold(value), state[1] + fold(value * normed[k, c, at, :].astype(F32))

        def keep_summed(at, value):
            dsum[c, at, :] = value
            low[k, c, at, :] = value.astype(BF16)

        norm_back(tiles(sums, (zero, zero)), normed.at[k, c], inv1[k, c], keep_summed)
        mix_send(low.at[k, c], 2 * blocks - 1 - k, c)

    def peer_forward(k, c):
        if k == 0:
            pair(0, k, c).wait_recv()
        else:
            team_all(k, c).wait()
            pair(2, k, c).wait()

            def add(at, state):
                value = normed_p[k, c, at, :].astype(F32) + dhid_p[c, at, :].astype(F32)
                tmp[at, :] = value
                return state + fold(value)

            norm_tmp(tiles(add, zero), inv_p, normed_p.at[k, c])
        matmul(wit.at[k], normed_p.at[k, c], to_tmp)

        def gelu(at, state):
            first, second = gelu_parts(tmp[at, :])
            recv[k, c, at, :] = first.astype(BF16)
            deriv_p[k, c, at, :] = second.astype(BF16)
            return state

        tiles(gelu)
        matmul(wot.at[k], recv.at[k, c], to_tmp)

        def skip(at, state):
            value = tmp[at, :] + normed_p[k, c, at, :].astype(F32)
            tmp[at, :] = value
            return state + fold(value)

        norm_tmp(tiles(skip, zero), inv_p, dhid_p.at[c])
        if k < blocks - 1:
            team_send(k + 1, c)
            return
        pair(1, k, c).wait_recv()

        def upward(at, state):
            value = dsl_p[k, c, at, :].astype(F32)
            tmp[at, :] = value
            return state[0] + fold(value), state[1] + fold(value * dhid_p[c, at, :].astype(F32))

        def keep(at, value):
            dsl_p[k, c, at, :] = value.astype(BF16)

        norm_back(tiles(upward, (zero, zero)), dhid_p.at[c], inv_p[...], keep)

    def peer_backward(k, c):
        if k < blocks - 1:
            pair(1, k, c).wait_recv()

        def sink(at, value):
            dhid_p[c, at, :] = (value * deriv_p[k, c, at, :].astype(F32)).astype(BF16)

        matmul(wo.at[k], dsl_p.at[k, c], sink)

    def outer(left, right):
        return lax.dot_general(left, right, (((1,), (1,)), ((), ())), preferred_element_type=F32)

    part = pl.ds(pl.multiple_of(mine * half, half), half)

    def bands(size, body):
        def step(i, carry):
            body(i * span)
            return carry

        lax.fori_loop(0, size // span, step, 0)

    def band(start):
        return pl.ds(pl.multiple_of(start, span), span)

    def own_grads(k):
        def first(start):
            src = band(mine * half + start)
            total = sum(outer(normed[k, c, src, :], dhid[k, c]) for c in range(cuts))
            gi_s[k, 0, band(start), :] = total.astype(BF16)

        bands(half, first)

        def second(start):
            at = band(start)
            total = sum(outer(act[k, c, at, :], dsl[k, c, part, :]) for c in range(cuts))
            go_s[k, 0, at, :] = total.astype(BF16)

        bands(hid, second)

    def peer_grads(k):
        def put(out, at, total):
            out[k, 0, at, :] = (out[k, 0, at, :].astype(F32) + total.astype(BF16).astype(F32)).astype(BF16)

        def first(start):
            src = band(mine * half + start)
            put(gi_s, band(start), sum(outer(normed_p[k, c, src, :], dhid_p[c]) for c in range(cuts)))

        bands(half, first)

        def second(start):
            at = band(start)
            put(go_s, at, sum(outer(recv[k, c, at, :], dsl_p[k, c, part, :]) for c in range(cuts)))

        bands(hid, second)

    def each(body):
        def step(c, carry):
            body(c)
            return carry

        lax.fori_loop(0, cuts, step, 0)

    for c in range(cuts):
        loads[c].wait()
        mix_send(x_in.at[c], 0, c)
    for c in range(cuts):
        loads[cuts + c].wait()
    pair_send(1, blocks - 1, 0)
    for load in loads[2 * cuts:]:
        load.wait()
    edge = min(256, width, hid)

    def flip(i, carry):
        a = pl.ds(pl.multiple_of(lax.rem(i, hid // edge) * edge, edge), edge)
        for k in range(blocks):
            for j in range(width // edge):
                b = pl.ds(j * edge, edge)
                wit[k, a, b] = wi[k, b, a].T
                wot[k, b, a] = wo[k, a, b].T
        return carry

    lax.fori_loop(0, hid // edge, flip, 0)

    def ahead(k, c):
        if k > 0:
            peer_forward(k - 1, c)
        mix_all(k, c).wait_recv()
        if k > 0:
            pair_part(2, k, c, far).start()
        forward(k, c)
        if k < blocks - 1:
            mix_send(x_hat.at[k, c], k + 1, c)
        else:
            backward(k, c)

    def last_ahead(c):
        peer_forward(blocks - 1, c)
        peer_backward(blocks - 1, c)
        mix_all(blocks, c).wait_recv()
        backward(blocks - 2, c)

    def finish(c):
        mix_all(2 * blocks - 1, c).wait_recv()

        def write(at, state):
            orow[0, at, pl.ds(c * rows, rows)] = (dsum[c, at, :] + recv[2 * blocks - 1, c, at, :].astype(F32)).astype(BF16)
            return state

        tiles(write)

    each(functools.partial(ahead, 0))
    for c in range(1, cuts):
        pair_send(1, blocks - 1, c)
    for k in range(1, blocks):
        each(functools.partial(ahead, k))
    own_grads(blocks - 1)
    each(last_ahead)
    peer_grads(blocks - 1)
    for k in reversed(range(blocks - 1)):
        own_grads(k)
        each(functools.partial(peer_backward, k))
        peer_grads(k)
    for c in range(cuts):
        finish(c)
    for c in range(cuts):
        pair(0, 0, c).wait_send()
        for k in range(blocks):
            pair(1, k, c).wait_send()
        for m in range(2 * blocks):
            mix_all(m, c).wait_send()


def store(count, *refs):
    sem = refs[-1]
    moves = []
    for src, dst in zip(refs[:count], refs[count:2 * count]):
        for k in range(src.shape[0]):
            for r in range(4):
                step = src.shape[-2] // 4
                at = (k,) + (0,) * (len(src.shape) - 3) + (pl.ds(r * step, step),)
                moves.append(pltpu.make_async_copy(src.at[at], dst.at[at], sem.at[len(moves)]))
    for move in moves:
        move.start()
    for move in moves:
        move.wait()


def written(values):
    count = len(values)
    pieces = sum(4 * v.shape[0] for v in values)
    return pl.pallas_call(
        functools.partial(store, count),
        out_shape=tuple(jax.ShapeDtypeStruct(v.shape, v.dtype) for v in values),
        in_specs=[pl.BlockSpec(memory_space=pltpu.VMEM)] * count,
        out_specs=[pl.BlockSpec(memory_space=pl.ANY)] * count,
        scratch_shapes=[pltpu.SemaphoreType.DMA((pieces,))],
        compiler_params=pltpu.CompilerParams(vmem_limit_bytes=1024 * 1024),
    )(*values)


def per_device(n_tok, n_dp, row_input, out_grad, in_weight, out_weight):
    blocks, _, width, hid = in_weight.shape
    row_count = row_input.shape[2]
    cuts = max(1, row_count // 256)
    rows = row_count // cuts
    half = width // n_dp
    wide = (cuts, width, rows)
    deep = (cuts, hid, rows)
    vm = pltpu.VMEM
    dma = pltpu.SemaphoreType.DMA
    return written(pl.pallas_call(
        functools.partial(kernel, n_tok, n_dp, cuts, 64, 256, width),
        out_shape=(
            pltpu.VMEM(row_input.shape, BF16),
            pltpu.VMEM((blocks, 1, half, hid), BF16),
            pltpu.VMEM((blocks, 1, hid, half), BF16),
        ),
        in_specs=[pl.BlockSpec(memory_space=pl.ANY)] * 4,
        out_specs=[pl.BlockSpec(memory_space=pltpu.VMEM)] * 3,
        scratch_shapes=[
            vm(wide, BF16),
            vm((blocks,) + wide, BF16),
            vm((2 * blocks,) + wide, BF16),
            vm(wide, BF16),
            vm((blocks, width, hid), BF16),
            vm((blocks, hid, width), BF16),
            vm((blocks, hid, width), BF16),
            vm((blocks, width, hid), BF16),
            vm((blocks,) + wide, BF16),
            vm((blocks,) + deep, BF16),
            vm((blocks,) + deep, F32),
            vm((blocks,) + wide, BF16),
            vm((blocks,) + deep, BF16),
            vm((blocks,) + wide, BF16),
            vm(wide, F32),
            vm((blocks,) + wide, BF16),
            vm((blocks,) + wide, BF16),
            vm((blocks,) + deep, BF16),
            vm(deep, BF16),
            vm((width, rows), F32),
            vm((blocks, cuts, 1, rows), F32),
            vm((blocks, cuts, 1, rows), F32),
            vm((1, rows), F32),
            dma((2 * cuts + 2 * blocks,)),
            dma((2 * blocks, cuts)),
            dma((2 * blocks, cuts)),
            dma((3, blocks, cuts)),
            dma((3, blocks, cuts)),
            dma((blocks, cuts)),
            dma((blocks, cuts)),
        ],
        compiler_params=pltpu.CompilerParams(
            collective_id=0, has_side_effects=True, vmem_limit_bytes=57 * 1024 * 1024
        ),
    )(row_input, out_grad, in_weight, out_weight))


def solution(mesh):
    return jax.shard_map(
        functools.partial(per_device, mesh.shape["tok"], mesh.shape["dp"]),
        mesh=mesh,
        in_specs=(
            P("tok", None, "dp"),
            P("tok", None, "dp"),
            P(None, "tok", None, None),
            P(None, "tok", None, None),
        ),
        out_specs=(P("tok", None, "dp"), P(None, "tok", "dp", None), P(None, "tok", None, "dp")),
        check_vma=False,
    )
```

```python
import functools

import jax
import jax.numpy as jnp
from jax import lax
from jax.experimental import pallas as pl
from jax.experimental.pallas import tpu as pltpu
from jax.sharding import PartitionSpec as P

epsilon = 1e-05
MESH = pl.DeviceIdType.MESH
F32 = jnp.float32
BF16 = jnp.bfloat16


def gelu_parts(hidden):
    cumulative = 0.5 * (1.0 + lax.erf(hidden * 0.7071067811865476))
    density = jnp.exp(-0.5 * hidden * hidden) * 0.3989422804014327
    return (hidden * cumulative, cumulative + hidden * density)


def kernel(
    n_tok, n_dp, cuts, tile, span, piece,
    x_hbm, g_hbm, wi_hbm, wo_hbm,
    gi_s, go_s, dsum, last,
    x_in, x_hat, recv, grad, wi, wo, wit, wot, normed, act, deriv, dsl, dhid, low,
    normed_p, dsl_p, deriv_p, dhid_p, tmp, inv1, inv2, inv_p,
    ld_sem, z_send, z_recv, x_send, x_recv, p_send, p_recv,
):
    blocks, width, hid = wi.shape
    rows = x_in.shape[2]
    head = width // n_tok
    half = width // n_dp
    me = lax.axis_index("tok")
    mine = lax.axis_index("dp")
    other = lax.rem(mine + 1, n_dp)

    barrier = pltpu.get_barrier_semaphore()

    def greet(i, carry):
        peer = lax.rem(me + 1 + i, n_tok)
        pl.semaphore_signal(barrier, inc=1, device_id={"tok": peer}, device_id_type=MESH)
        return carry

    lax.fori_loop(0, n_tok - 1, greet, 0)
    pl.semaphore_signal(barrier, inc=1, device_id={"dp": other}, device_id_type=MESH)

    loads = []
    for c in range(cuts):
        loads.append(pltpu.make_async_copy(x_hbm.at[0, :, pl.ds(c * rows, rows)], x_in.at[c], ld_sem.at[c]))
    for c in range(cuts):
        loads.append(pltpu.make_async_copy(g_hbm.at[0, :, pl.ds(c * rows, rows)], grad.at[c], ld_sem.at[cuts + c]))
    for k in range(blocks):
        loads.append(pltpu.make_async_copy(wi_hbm.at[k, 0], wi.at[k], ld_sem.at[2 * cuts + 2 * k]))
        loads.append(pltpu.make_async_copy(wo_hbm.at[k, 0], wo.at[k], ld_sem.at[2 * cuts + 2 * k + 1]))
    for load in loads:
        load.start()

    pl.semaphore_wait(barrier, n_tok)

    team = n_tok // 2
    base = (me // team) * team
    lower = base == 0
    outer_half = jnp.where(lower, me, n_tok - 1 - me) < team // 2

    def spot(i):
        if team % 4:
            return i
        return i - lax.rem(i, 4) + 2 * lax.rem(i, 2) + lax.div(lax.rem(i, 4), 2)

    def land(m):
        return last if m == 2 * blocks - 1 else recv.at[m]

    def mix_send(src, m, c):
        def go(peer):
            pltpu.make_async_remote_copy(
                src_ref=src.at[pl.ds(pl.multiple_of(peer * head, head), head)],
                dst_ref=land(m).at[c, pl.ds(pl.multiple_of(me * head, head), head)],
                send_sem=z_send.at[m, c],
                recv_sem=z_recv.at[m, c],
                device_id={"tok": peer},
                device_id_type=MESH,
            ).start()

        def cross(i, carry):
            at = spot(i)
            go(jnp.where(lower, n_tok - 1 - at, at))
            return carry

        def local(i, carry):
            at = spot(lax.rem(i + team // 2, team))
            peer = jnp.where(lower, at, n_tok - 1 - at)
            pl.when(peer != me)(functools.partial(go, peer))
            return carry

        @pl.when(outer_half)
        def _():
            lax.fori_loop(0, team, lambda i, carry: local(i, cross(i, carry)), 0)

        @pl.when(jnp.logical_not(outer_half))
        def _():
            lax.fori_loop(0, team, cross, 0)
            lax.fori_loop(0, team, local, 0)

        own = pl.ds(pl.multiple_of(me * head, head), head)
        land(m)[c, own, :] = src[own, :]

    def mix_all(m, c):
        part = land(m).at[c, pl.ds(0, head * (n_tok - 1))]
        return pltpu.make_async_remote_copy(
            src_ref=part, dst_ref=part, send_sem=z_send.at[m, c], recv_sem=z_recv.at[m, c],
            device_id={"tok": lax.rem(me + 1, n_tok)}, device_id_type=MESH,
        )

    far = pl.ds(pl.multiple_of((team - base) * head, head), team * head)

    def team_send(k, c):
        def one(i, carry):
            peer = base + lax.rem(me - base + 1 + i, team)
            pltpu.make_async_remote_copy(
                src_ref=dhid_p.at[c, pl.ds(pl.multiple_of(peer * head, head), head)],
                dst_ref=normed_p.at[k, c, pl.ds(pl.multiple_of(me * head, head), head)],
                send_sem=p_send.at[k, c],
                recv_sem=p_recv.at[k, c],
                device_id={"tok": peer},
                device_id_type=MESH,
            ).start()
            return carry

        lax.fori_loop(0, team - 1, one, 0)
        own = pl.ds(pl.multiple_of(me * head, head), head)
        normed_p[k, c, own, :] = dhid_p[c, own, :]

    def team_all(k, c):
        part = normed_p.at[k, c, pl.ds(0, head * (team - 1))]
        return pltpu.make_async_remote_copy(
            src_ref=part, dst_ref=part, send_sem=p_send.at[k, c], recv_sem=p_recv.at[k, c],
            device_id={"tok": lax.rem(me + 1, n_tok)}, device_id_type=MESH,
        )

    def pair_part(kind, k, c, at):
        if kind == 0:
            src, dst = normed.at[k, c], normed_p.at[k, c]
        elif kind == 2:
            src, dst = recv.at[k, c], normed_p.at[k, c]
        else:
            src, dst = grad.at[c] if k == blocks - 1 else dsl.at[k, c], dsl_p.at[k, c]
        return pltpu.make_async_remote_copy(
            src_ref=src.at[at], dst_ref=dst.at[at],
            send_sem=x_send.at[kind, k, c], recv_sem=x_recv.at[kind, k, c],
            device_id={"dp": other}, device_id_type=MESH,
        )

    def pair(kind, k, c):
        return pair_part(kind, k, c, far if kind == 2 else pl.ds(0, width))

    def pair_send(kind, k, c):
        def one(i, carry):
            pair_part(kind, k, c, pl.ds(pl.multiple_of(i * piece, piece), piece)).start()
            return carry

        lax.fori_loop(0, width // piece, one, 0)

    def tiles(body, carry=0):
        def step(i, state):
            return body(pl.ds(pl.multiple_of(i * tile, tile), tile), state)

        return lax.fori_loop(0, width // tile, step, carry)

    zero = jnp.zeros((8, rows), F32)

    def fold(value):
        return jnp.sum(value.reshape(tile // 8, 8, rows), axis=0)

    def mean(total):
        return jnp.sum(total, axis=0, keepdims=True) * (1.0 / width)

    stride = min(2 * span, width)

    def matmul(left, right, sink):
        def step(i, carry):
            at = pl.ds(pl.multiple_of(i * stride, stride), stride)
            sink(at, jnp.dot(left[at, :], right[...], preferred_element_type=F32))
            return carry

        lax.fori_loop(0, left.shape[0] // stride, step, 0)

    def to_tmp(at, value):
        tmp[at, :] = value

    def norm_tmp(total, inv_ref, out_ref):
        center = mean(total)

        def spread(at, state):
            gap = tmp[at, :] - center
            return state + fold(gap * gap)

        inverse = lax.rsqrt(mean(tiles(spread, zero)) + epsilon)
        inv_ref[...] = inverse

        def write(at, state):
            out_ref[at, :] = ((tmp[at, :] - center) * inverse).astype(BF16)
            return state

        tiles(write)

    def forward(k, c):
        current = x_in.at[c] if k == 0 else x_hat.at[k - 1, c]

        def add(at, state):
            value = recv[k, c, at, :].astype(F32) + current[at, :].astype(F32)
            tmp[at, :] = value
            return state + fold(value)

        norm_tmp(tiles(add, zero), inv1.at[k, c], normed.at[k, c])
        if k == 0:
            pair_send(0, k, c)
        matmul(wit.at[k], normed.at[k, c], to_tmp)

        def gelu(at, state):
            first, second = gelu_parts(tmp[at, :])
            act[k, c, at, :] = first.astype(BF16)
            deriv[k, c, at, :] = second
            return state

        tiles(gelu)
        matmul(wot.at[k], act.at[k, c], to_tmp)

        def skip(at, state):
            value = tmp[at, :] + normed[k, c, at, :].astype(F32)
            tmp[at, :] = value
            return state + fold(value)

        norm_tmp(tiles(skip, zero), inv2.at[k, c], x_hat.at[k, c])

    def norm_back(means, hat, inverse, sink):
        up, cross = mean(means[0]), mean(means[1])

        def write(at, state):
            value = inverse * (tmp[at, :] - up - hat[at, :].astype(F32) * cross)
            sink(at, value)
            return state

        tiles(write)

    def backward(k, c):
        def upward(at, state):
            if k == blocks - 1:
                value = grad[c, at, :].astype(F32)
            else:
                value = dsum[c, at, :] + recv[2 * blocks - 2 - k, c, at, :].astype(F32)
                value = value.astype(BF16).astype(F32)
            tmp[at, :] = value
            return state[0] + fold(value), state[1] + fold(value * x_hat[k, c, at, :].astype(F32))

        def keep_second(at, value):
            tmp[at, :] = value
            dsl[k, c, at, :] = value.astype(BF16)

        norm_back(tiles(upward, (zero, zero)), x_hat.at[k, c], inv2[k, c], keep_second)
        if k < blocks - 1:
            pair_send(1, k, c)

        def hidden_sink(at, value):
            dhid[k, c, at, :] = (value * deriv[k, c, at, :]).astype(BF16)

        matmul(wo.at[k], dsl.at[k, c], hidden_sink)

        def add_tmp(at, value):
            tmp[at, :] = tmp[at, :] + value

        matmul(wi.at[k], dhid.at[k, c], add_tmp)

        def sums(at, state):
            value = tmp[at, :]
            return state[0] + fold(value), state[1] + fold(value * normed[k, c, at, :].astype(F32))

        def keep_summed(at, value):
            dsum[c, at, :] = value
            low[k, c, at, :] = value.astype(BF16)

        norm_back(tiles(sums, (zero, zero)), normed.at[k, c], inv1[k, c], keep_summed)
        mix_send(low.at[k, c], 2 * blocks - 1 - k, c)

    def peer_forward(k, c):
        if k == 0:
            pair(0, k, c).wait_recv()
        else:
            team_all(k, c).wait()
            pair(2, k, c).wait()

            def add(at, state):
                value = normed_p[k, c, at, :].astype(F32) + dhid_p[c, at, :].astype(F32)
                tmp[at, :] = value
                return state + fold(value)

            norm_tmp(tiles(add, zero), inv_p, normed_p.at[k, c])
        matmul(wit.at[k], normed_p.at[k, c], to_tmp)

        def gelu(at, state):
            first, second = gelu_parts(tmp[at, :])
            recv[k, c, at, :] = first.astype(BF16)
            deriv_p[k, c, at, :] = second.astype(BF16)
            return state

        tiles(gelu)
        matmul(wot.at[k], recv.at[k, c], to_tmp)

        def skip(at, state):
            value = tmp[at, :] + normed_p[k, c, at, :].astype(F32)
            tmp[at, :] = value
            return state + fold(value)

        norm_tmp(tiles(skip, zero), inv_p, dhid_p.at[c])
        if k < blocks - 1:
            team_send(k + 1, c)
            return
        pair(1, k, c).wait_recv()

        def upward(at, state):
            value = dsl_p[k, c, at, :].astype(F32)
            tmp[at, :] = value
            return state[0] + fold(value), state[1] + fold(value * dhid_p[c, at, :].astype(F32))

        def keep(at, value):
            dsl_p[k, c, at, :] = value.astype(BF16)

        norm_back(tiles(upward, (zero, zero)), dhid_p.at[c], inv_p[...], keep)

    def peer_backward(k, c):
        if k < blocks - 1:
            pair(1, k, c).wait_recv()

        def sink(at, value):
            dhid_p[c, at, :] = (value * deriv_p[k, c, at, :].astype(F32)).astype(BF16)

        matmul(wo.at[k], dsl_p.at[k, c], sink)

    def outer(left, right):
        return lax.dot_general(left, right, (((1,), (1,)), ((), ())), preferred_element_type=F32)

    part = pl.ds(pl.multiple_of(mine * half, half), half)

    wide_span = min(2 * span, half, hid)

    def bands(size, body):
        def step(i, carry):
            body(i * wide_span)
            return carry

        lax.fori_loop(0, size // wide_span, step, 0)

    def band(start):
        return pl.ds(pl.multiple_of(start, wide_span), wide_span)

    def own_grads(k):
        def first(start):
            src = band(mine * half + start)
            total = sum(outer(normed[k, c, src, :], dhid[k, c]) for c in range(cuts))
            gi_s[k, 0, band(start), :] = total.astype(BF16)

        bands(half, first)

        def second(start):
            at = band(start)
            total = sum(outer(act[k, c, at, :], dsl[k, c, part, :]) for c in range(cuts))
            go_s[k, 0, at, :] = total.astype(BF16)

        bands(hid, second)

    def peer_grads(k):
        def put(out, at, total):
            out[k, 0, at, :] = (out[k, 0, at, :].astype(F32) + total.astype(BF16).astype(F32)).astype(BF16)

        def first(start):
            src = band(mine * half + start)
            put(gi_s, band(start), sum(outer(normed_p[k, c, src, :], dhid_p[c]) for c in range(cuts)))

        bands(half, first)

        def second(start):
            at = band(start)
            put(go_s, at, sum(outer(recv[k, c, at, :], dsl_p[k, c, part, :]) for c in range(cuts)))

        bands(hid, second)

    def each(body):
        def step(c, carry):
            body(c)
            return carry

        lax.fori_loop(0, cuts, step, 0)

    for c in range(cuts):
        loads[c].wait()
        mix_send(x_in.at[c], 0, c)
    for c in range(cuts):
        loads[cuts + c].wait()
    pair_send(1, blocks - 1, 0)
    for load in loads[2 * cuts:]:
        load.wait()
    edge = min(256, width, hid)

    def flip(i, carry):
        a = pl.ds(pl.multiple_of(lax.rem(i, hid // edge) * edge, edge), edge)
        for k in range(blocks):
            for j in range(width // edge):
                b = pl.ds(j * edge, edge)
                wit[k, a, b] = wi[k, b, a].T
                wot[k, b, a] = wo[k, a, b].T
        return carry

    lax.fori_loop(0, hid // edge, flip, 0)

    def ahead(k, c):
        if k > 0:
            peer_forward(k - 1, c)
        mix_all(k, c).wait_recv()
        if k > 0:
            pair_part(2, k, c, far).start()
        forward(k, c)
        if k < blocks - 1:
            mix_send(x_hat.at[k, c], k + 1, c)
        else:
            backward(k, c)

    def last_ahead(c):
        peer_forward(blocks - 1, c)
        peer_backward(blocks - 1, c)
        mix_all(blocks, c).wait_recv()
        backward(blocks - 2, c)

    each(functools.partial(ahead, 0))
    for c in range(1, cuts):
        pair_send(1, blocks - 1, c)
    for k in range(1, blocks):
        each(functools.partial(ahead, k))
    own_grads(blocks - 1)
    each(last_ahead)
    peer_grads(blocks - 1)
    for k in reversed(range(blocks - 1)):
        own_grads(k)
        each(functools.partial(peer_backward, k))
        peer_grads(k)
    for c in range(cuts):
        mix_all(2 * blocks - 1, c).wait_recv()
        pair(0, 0, c).wait_send()
        for k in range(blocks):
            pair(1, k, c).wait_send()
        for m in range(2 * blocks):
            mix_all(m, c).wait_send()


def store(gi, go, dsum, last, orow_hbm, gi_hbm, go_hbm, orow, sem):
    cuts, width, rows = dsum.shape
    tile, parts = 64, 4
    moves = []

    def move(src, dst):
        moves.append(pltpu.make_async_copy(src, dst, sem.at[len(moves)]))
        moves[-1].start()

    for src, dst in ((gi, gi_hbm), (go, go_hbm)):
        for k in range(src.shape[0]):
            step = src.shape[2] // parts
            for r in range(parts):
                at = pl.ds(r * step, step)
                move(src.at[k, 0, at], dst.at[k, 0, at])
    step = width // parts
    for r in range(parts):
        def write(i, carry):
            at = pl.ds(pl.multiple_of(r * step + i * tile, tile), tile)
            for c in range(cuts):
                orow[at, pl.ds(c * rows, rows)] = (dsum[c, at, :] + last[c, at, :].astype(F32)).astype(BF16)
            return carry

        lax.fori_loop(0, step // tile, write, 0)
        at = pl.ds(r * step, step)
        move(orow.at[at], orow_hbm.at[0, at])
    for done in moves:
        done.wait()


def written(gi, go, dsum, last):
    cuts, width, rows = dsum.shape
    shape = (1, width, cuts * rows)
    return pl.pallas_call(
        store,
        out_shape=tuple(jax.ShapeDtypeStruct(t, BF16) for t in (shape, gi.shape, go.shape)),
        in_specs=[pl.BlockSpec(memory_space=pltpu.VMEM)] * 4,
        out_specs=[pl.BlockSpec(memory_space=pl.ANY)] * 3,
        scratch_shapes=[pltpu.VMEM(shape[1:], BF16), pltpu.SemaphoreType.DMA((4 + 8 * gi.shape[0],))],
        compiler_params=pltpu.CompilerParams(vmem_limit_bytes=2 * 1024 * 1024),
    )(gi, go, dsum, last)


def per_device(n_tok, n_dp, row_input, out_grad, in_weight, out_weight):
    blocks, _, width, hid = in_weight.shape
    row_count = row_input.shape[2]
    cuts = max(1, row_count // 256)
    rows = row_count // cuts
    half = width // n_dp
    wide = (cuts, width, rows)
    deep = (cuts, hid, rows)
    vm = pltpu.VMEM
    dma = pltpu.SemaphoreType.DMA
    return written(*pl.pallas_call(
        functools.partial(kernel, n_tok, n_dp, cuts, 64, 256, width),
        out_shape=(
            pltpu.VMEM((blocks, 1, half, hid), BF16),
            pltpu.VMEM((blocks, 1, hid, half), BF16),
            pltpu.VMEM(wide, F32),
            pltpu.VMEM(wide, BF16),
        ),
        in_specs=[pl.BlockSpec(memory_space=pl.ANY)] * 4,
        out_specs=[pl.BlockSpec(memory_space=pltpu.VMEM)] * 4,
        scratch_shapes=[
            vm(wide, BF16),
            vm((blocks,) + wide, BF16),
            vm((2 * blocks - 1,) + wide, BF16),
            vm(wide, BF16),
            vm((blocks, width, hid), BF16),
            vm((blocks, hid, width), BF16),
            vm((blocks, hid, width), BF16),
            vm((blocks, width, hid), BF16),
            vm((blocks,) + wide, BF16),
            vm((blocks,) + deep, BF16),
            vm((blocks,) + deep, F32),
            vm((blocks,) + wide, BF16),
            vm((blocks,) + deep, BF16),
            vm((blocks,) + wide, BF16),
            vm((blocks,) + wide, BF16),
            vm((blocks,) + wide, BF16),
            vm((blocks,) + deep, BF16),
            vm(deep, BF16),
            vm((width, rows), F32),
            vm((blocks, cuts, 1, rows), F32),
            vm((blocks, cuts, 1, rows), F32),
            vm((1, rows), F32),
            dma((2 * cuts + 2 * blocks,)),
            dma((2 * blocks, cuts)),
            dma((2 * blocks, cuts)),
            dma((3, blocks, cuts)),
            dma((3, blocks, cuts)),
            dma((blocks, cuts)),
            dma((blocks, cuts)),
        ],
        compiler_params=pltpu.CompilerParams(
            collective_id=0, has_side_effects=True, vmem_limit_bytes=54 * 1024 * 1024
        ),
    )(row_input, out_grad, in_weight, out_weight))


def solution(mesh):
    return jax.shard_map(
        functools.partial(per_device, mesh.shape["tok"], mesh.shape["dp"]),
        mesh=mesh,
        in_specs=(
            P("tok", None, "dp"),
            P("tok", None, "dp"),
            P(None, "tok", None, None),
            P(None, "tok", None, None),
        ),
        out_specs=(P("tok", None, "dp"), P(None, "tok", "dp", None), P(None, "tok", None, "dp")),
        check_vma=False,
    )
```

```python
import functools

import jax
import jax.numpy as jnp
from jax import lax
from jax.experimental import pallas as pl
from jax.experimental.pallas import tpu as pltpu
from jax.sharding import PartitionSpec as P

epsilon = 1e-05
MESH = pl.DeviceIdType.MESH
F32 = jnp.float32
BF16 = jnp.bfloat16


def gelu_parts(hidden):
    cumulative = 0.5 * (1.0 + lax.erf(hidden * 0.7071067811865476))
    density = jnp.exp(-0.5 * hidden * hidden) * 0.3989422804014327
    return (hidden * cumulative, cumulative + hidden * density)


def kernel(
    n_tok, n_dp, cuts, tile, span, piece,
    x_hbm, g_hbm, wi_hbm, wo_hbm,
    gi_s, go_s, dsum, last,
    x_in, x_hat, recv, grad, wi, wo, wit, wot, normed, act, deriv, dsl, dhid, low,
    normed_p, dsl_p, deriv_p, dhid_p, tmp, inv1, inv2, inv_p,
    ld_sem, z_send, z_recv, x_send, x_recv, p_send, p_recv, all_in,
):
    blocks, width, hid = wi.shape
    rows = x_in.shape[2]
    head = width // n_tok
    half = width // n_dp
    me = lax.axis_index("tok")
    mine = lax.axis_index("dp")
    other = lax.rem(mine + 1, n_dp)

    barrier = pltpu.get_barrier_semaphore()

    late = n_tok - n_tok // 4
    gate = late - 1

    def greet(i, carry):
        peer = lax.rem(me + 1 + i, n_tok)

        @pl.when((me < late) | (peer >= gate))
        def _():
            pl.semaphore_signal(barrier, inc=1, device_id={"tok": peer}, device_id_type=MESH)

        return carry

    lax.fori_loop(0, n_tok - 1, greet, 0)
    pl.semaphore_signal(barrier, inc=1, device_id={"dp": other}, device_id_type=MESH)

    loads = []
    for c in range(cuts):
        loads.append(pltpu.make_async_copy(x_hbm.at[0, :, pl.ds(c * rows, rows)], x_in.at[c], ld_sem.at[c]))
    for c in range(cuts):
        loads.append(pltpu.make_async_copy(g_hbm.at[0, :, pl.ds(c * rows, rows)], grad.at[c], ld_sem.at[cuts + c]))
    for k in range(blocks):
        loads.append(pltpu.make_async_copy(wi_hbm.at[k, 0], wi.at[k], ld_sem.at[2 * cuts + 2 * k]))
        loads.append(pltpu.make_async_copy(wo_hbm.at[k, 0], wo.at[k], ld_sem.at[2 * cuts + 2 * k + 1]))
    for load in loads:
        load.start()

    pl.semaphore_wait(barrier, jnp.where(me < gate, late, n_tok))

    @pl.when(me == gate)
    def _():
        def tell(i, carry):
            pl.semaphore_signal(all_in, inc=1, device_id={"tok": i}, device_id_type=MESH)
            return carry

        lax.fori_loop(0, gate, tell, 0)

    team = n_tok // 2
    base = (me // team) * team
    lower = base == 0
    outer_half = jnp.where(lower, me, n_tok - 1 - me) < team // 2

    def spot(i):
        if team % 4:
            return i
        return i - lax.rem(i, 4) + 2 * lax.rem(i, 2) + lax.div(lax.rem(i, 4), 2)

    def land(m):
        return last if m == 2 * blocks - 1 else recv.at[m]

    def turned(at, m, c):
        near = at >= team // 2
        return jnp.where(near & (lax.rem(jnp.int32(c + m), 2) == 1), team // 2 + team - 1 - at, at)

    def mix_send(src, m, c, turn=None):
        def go(peer):
            if turn is None:
                start(peer)
            else:
                pl.when((peer >= late) == (turn == 1))(functools.partial(start, peer))

        def start(peer):
            pltpu.make_async_remote_copy(
                src_ref=src.at[pl.ds(pl.multiple_of(peer * head, head), head)],
                dst_ref=land(m).at[c, pl.ds(pl.multiple_of(me * head, head), head)],
                send_sem=z_send.at[m, c],
                recv_sem=z_recv.at[m, c],
                device_id={"tok": peer},
                device_id_type=MESH,
            ).start()

        def cross(i, carry):
            at = turned(spot(i), m, c)
            go(jnp.where(lower, n_tok - 1 - at, at))
            return carry

        def local(i, carry):
            at = spot(lax.rem(i + team // 2, team))
            peer = jnp.where(lower, at, n_tok - 1 - at)
            pl.when(peer != me)(functools.partial(go, peer))
            return carry

        @pl.when(outer_half)
        def _():
            lax.fori_loop(0, team, lambda i, carry: local(i, cross(i, carry)), 0)

        @pl.when(jnp.logical_not(outer_half))
        def _():
            lax.fori_loop(0, team, cross, 0)
            lax.fori_loop(0, team, local, 0)

        if turn == 1:
            return
        own = pl.ds(pl.multiple_of(me * head, head), head)
        land(m)[c, own, :] = src[own, :]

    def mix_all(m, c):
        part = land(m).at[c, pl.ds(0, head * (n_tok - 1))]
        return pltpu.make_async_remote_copy(
            src_ref=part, dst_ref=part, send_sem=z_send.at[m, c], recv_sem=z_recv.at[m, c],
            device_id={"tok": lax.rem(me + 1, n_tok)}, device_id_type=MESH,
        )

    far = pl.ds(pl.multiple_of((team - base) * head, head), team * head)

    def team_send(k, c):
        def one(i, carry):
            peer = base + lax.rem(me - base + 1 + i, team)
            pltpu.make_async_remote_copy(
                src_ref=dhid_p.at[c, pl.ds(pl.multiple_of(peer * head, head), head)],
                dst_ref=normed_p.at[k, c, pl.ds(pl.multiple_of(me * head, head), head)],
                send_sem=p_send.at[k, c],
                recv_sem=p_recv.at[k, c],
                device_id={"tok": peer},
                device_id_type=MESH,
            ).start()
            return carry

        lax.fori_loop(0, team - 1, one, 0)
        own = pl.ds(pl.multiple_of(me * head, head), head)
        normed_p[k, c, own, :] = dhid_p[c, own, :]

    def team_all(k, c):
        part = normed_p.at[k, c, pl.ds(0, head * (team - 1))]
        return pltpu.make_async_remote_copy(
            src_ref=part, dst_ref=part, send_sem=p_send.at[k, c], recv_sem=p_recv.at[k, c],
            device_id={"tok": lax.rem(me + 1, n_tok)}, device_id_type=MESH,
        )

    def pair_part(kind, k, c, at):
        if kind == 0:
            src, dst = normed.at[k, c], normed_p.at[k, c]
        elif kind == 2:
            src, dst = recv.at[k, c], normed_p.at[k, c]
        else:
            src, dst = grad.at[c] if k == blocks - 1 else dsl.at[k, c], dsl_p.at[k, c]
        return pltpu.make_async_remote_copy(
            src_ref=src.at[at], dst_ref=dst.at[at],
            send_sem=x_send.at[kind, k, c], recv_sem=x_recv.at[kind, k, c],
            device_id={"dp": other}, device_id_type=MESH,
        )

    def pair(kind, k, c):
        return pair_part(kind, k, c, far if kind == 2 else pl.ds(0, width))

    def pair_send(kind, k, c):
        def one(i, carry):
            pair_part(kind, k, c, pl.ds(pl.multiple_of(i * piece, piece), piece)).start()
            return carry

        lax.fori_loop(0, width // piece, one, 0)

    def tiles(body, carry=0):
        def step(i, state):
            return body(pl.ds(pl.multiple_of(i * tile, tile), tile), state)

        return lax.fori_loop(0, width // tile, step, carry)

    zero = jnp.zeros((8, rows), F32)

    def fold(value):
        return jnp.sum(value.reshape(tile // 8, 8, rows), axis=0)

    def mean(total):
        return jnp.sum(total, axis=0, keepdims=True) * (1.0 / width)

    stride = min(2 * span, width)

    def matmul(left, right, sink):
        def step(i, carry):
            at = pl.ds(pl.multiple_of(i * stride, stride), stride)
            sink(at, jnp.dot(left[at, :], right[...], preferred_element_type=F32))
            return carry

        lax.fori_loop(0, left.shape[0] // stride, step, 0)

    def to_tmp(at, value):
        tmp[at, :] = value

    def norm_tmp(total, inv_ref, out_ref):
        center = mean(total)

        def spread(at, state):
            gap = tmp[at, :] - center
            return state + fold(gap * gap)

        inverse = lax.rsqrt(mean(tiles(spread, zero)) + epsilon)
        inv_ref[...] = inverse

        def write(at, state):
            out_ref[at, :] = ((tmp[at, :] - center) * inverse).astype(BF16)
            return state

        tiles(write)

    def forward(k, c):
        current = x_in.at[c] if k == 0 else x_hat.at[k - 1, c]

        def add(at, state):
            value = recv[k, c, at, :].astype(F32) + current[at, :].astype(F32)
            tmp[at, :] = value
            return state + fold(value)

        norm_tmp(tiles(add, zero), inv1.at[k, c], normed.at[k, c])
        if k == 0:
            pair_send(0, k, c)
        matmul(wit.at[k], normed.at[k, c], to_tmp)

        def gelu(at, state):
            first, second = gelu_parts(tmp[at, :])
            act[k, c, at, :] = first.astype(BF16)
            deriv[k, c, at, :] = second
            return state

        tiles(gelu)
        matmul(wot.at[k], act.at[k, c], to_tmp)

        def skip(at, state):
            value = tmp[at, :] + normed[k, c, at, :].astype(F32)
            tmp[at, :] = value
            return state + fold(value)

        norm_tmp(tiles(skip, zero), inv2.at[k, c], x_hat.at[k, c])

    def norm_back(means, hat, inverse, sink):
        up, cross = mean(means[0]), mean(means[1])

        def write(at, state):
            value = inverse * (tmp[at, :] - up - hat[at, :].astype(F32) * cross)
            sink(at, value)
            return state

        tiles(write)

    def backward(k, c):
        def upward(at, state):
            if k == blocks - 1:
                value = grad[c, at, :].astype(F32)
            else:
                value = dsum[c, at, :] + recv[2 * blocks - 2 - k, c, at, :].astype(F32)
                value = value.astype(BF16).astype(F32)
            tmp[at, :] = value
            return state[0] + fold(value), state[1] + fold(value * x_hat[k, c, at, :].astype(F32))

        def keep_second(at, value):
            tmp[at, :] = value
            dsl[k, c, at, :] = value.astype(BF16)

        norm_back(tiles(upward, (zero, zero)), x_hat.at[k, c], inv2[k, c], keep_second)
        if k < blocks - 1:
            pair_send(1, k, c)

        def hidden_sink(at, value):
            dhid[k, c, at, :] = (value * deriv[k, c, at, :]).astype(BF16)

        matmul(wo.at[k], dsl.at[k, c], hidden_sink)

        def add_tmp(at, value):
            tmp[at, :] = tmp[at, :] + value

        matmul(wi.at[k], dhid.at[k, c], add_tmp)

        def sums(at, state):
            value = tmp[at, :]
            return state[0] + fold(value), state[1] + fold(value * normed[k, c, at, :].astype(F32))

        def keep_summed(at, value):
            dsum[c, at, :] = value
            low[k, c, at, :] = value.astype(BF16)

        norm_back(tiles(sums, (zero, zero)), normed.at[k, c], inv1[k, c], keep_summed)
        mix_send(low.at[k, c], 2 * blocks - 1 - k, c)

    def peer_forward(k, c):
        if k == 0:
            pair(0, k, c).wait_recv()
        else:
            team_all(k, c).wait()
            pair(2, k, c).wait()

            def add(at, state):
                value = normed_p[k, c, at, :].astype(F32) + dhid_p[c, at, :].astype(F32)
                tmp[at, :] = value
                return state + fold(value)

            norm_tmp(tiles(add, zero), inv_p, normed_p.at[k, c])
        matmul(wit.at[k], normed_p.at[k, c], to_tmp)

        def gelu(at, state):
            first, second = gelu_parts(tmp[at, :])
            recv[k, c, at, :] = first.astype(BF16)
            deriv_p[k, c, at, :] = second.astype(BF16)
            return state

        tiles(gelu)
        matmul(wot.at[k], recv.at[k, c], to_tmp)

        def skip(at, state):
            value = tmp[at, :] + normed_p[k, c, at, :].astype(F32)
            tmp[at, :] = value
            return state + fold(value)

        norm_tmp(tiles(skip, zero), inv_p, dhid_p.at[c])
        if k < blocks - 1:
            team_send(k + 1, c)
            return
        pair(1, k, c).wait_recv()

        def upward(at, state):
            value = dsl_p[k, c, at, :].astype(F32)
            tmp[at, :] = value
            return state[0] + fold(value), state[1] + fold(value * dhid_p[c, at, :].astype(F32))

        def keep(at, value):
            dsl_p[k, c, at, :] = value.astype(BF16)

        norm_back(tiles(upward, (zero, zero)), dhid_p.at[c], inv_p[...], keep)

    def peer_backward(k, c):
        if k < blocks - 1:
            pair(1, k, c).wait_recv()

        def sink(at, value):
            dhid_p[c, at, :] = (value * deriv_p[k, c, at, :].astype(F32)).astype(BF16)

        matmul(wo.at[k], dsl_p.at[k, c], sink)

    def outer(left, right):
        return lax.dot_general(left, right, (((1,), (1,)), ((), ())), preferred_element_type=F32)

    part = pl.ds(pl.multiple_of(mine * half, half), half)

    wide_span = min(2 * span, half, hid)

    def bands(size, body):
        def step(i, carry):
            body(i * wide_span)
            return carry

        lax.fori_loop(0, size // wide_span, step, 0)

    def band(start):
        return pl.ds(pl.multiple_of(start, wide_span), wide_span)

    def own_grads(k):
        def first(start):
            src = band(mine * half + start)
            total = sum(outer(normed[k, c, src, :], dhid[k, c]) for c in range(cuts))
            gi_s[k, 0, band(start), :] = total.astype(BF16)

        bands(half, first)

        def second(start):
            at = band(start)
            total = sum(outer(act[k, c, at, :], dsl[k, c, part, :]) for c in range(cuts))
            go_s[k, 0, at, :] = total.astype(BF16)

        bands(hid, second)

    def peer_grads(k):
        def put(out, at, total):
            out[k, 0, at, :] = (out[k, 0, at, :].astype(F32) + total.astype(BF16).astype(F32)).astype(BF16)

        def first(start):
            src = band(mine * half + start)
            put(gi_s, band(start), sum(outer(normed_p[k, c, src, :], dhid_p[c]) for c in range(cuts)))

        bands(half, first)

        def second(start):
            at = band(start)
            put(go_s, at, sum(outer(recv[k, c, at, :], dsl_p[k, c, part, :]) for c in range(cuts)))

        bands(hid, second)

    def each(body):
        def step(c, carry):
            body(c)
            return carry

        lax.fori_loop(0, cuts, step, 0)

    for c in range(cuts):
        loads[c].wait()
        if c > 0:
            mix_send(x_in.at[c], 0, c)
            continue
        mix_send(x_in.at[c], 0, c, 0)

        @pl.when(me < gate)
        def _():
            pl.semaphore_wait(all_in, 1)

        mix_send(x_in.at[c], 0, c, 1)
    for c in range(cuts):
        loads[cuts + c].wait()
    pair_send(1, blocks - 1, 0)
    for load in loads[2 * cuts:]:
        load.wait()
    edge = min(256, width, hid)

    def flip(i, carry):
        a = pl.ds(pl.multiple_of(lax.rem(i, hid // edge) * edge, edge), edge)
        for k in range(blocks):
            for j in range(width // edge):
                b = pl.ds(j * edge, edge)
                wit[k, a, b] = wi[k, b, a].T
                wot[k, b, a] = wo[k, a, b].T
        return carry

    lax.fori_loop(0, hid // edge, flip, 0)

    def ahead(k, c):
        if k > 0:
            peer_forward(k - 1, c)
        mix_all(k, c).wait_recv()
        if k > 0:
            pair_part(2, k, c, far).start()
        forward(k, c)
        if k < blocks - 1:
            mix_send(x_hat.at[k, c], k + 1, c)
        else:
            backward(k, c)

    def last_ahead(c):
        peer_forward(blocks - 1, c)
        peer_backward(blocks - 1, c)
        mix_all(blocks, c).wait_recv()
        backward(blocks - 2, c)

    each(functools.partial(ahead, 0))
    for c in range(1, cuts):
        pair_send(1, blocks - 1, c)
    for k in range(1, blocks):
        each(functools.partial(ahead, k))
    own_grads(blocks - 1)
    each(last_ahead)
    peer_grads(blocks - 1)
    for k in reversed(range(blocks - 1)):
        own_grads(k)
        each(functools.partial(peer_backward, k))
        peer_grads(k)
    for c in range(cuts):
        mix_all(2 * blocks - 1, c).wait_recv()
        pair(0, 0, c).wait_send()
        for k in range(blocks):
            pair(1, k, c).wait_send()
        for m in range(2 * blocks):
            mix_all(m, c).wait_send()


def store(gi, go, dsum, last, orow_hbm, gi_hbm, go_hbm, orow, sem):
    cuts, width, rows = dsum.shape
    tile, parts = 64, 4
    moves = []

    def move(src, dst):
        moves.append(pltpu.make_async_copy(src, dst, sem.at[len(moves)]))
        moves[-1].start()

    for src, dst in ((gi, gi_hbm), (go, go_hbm)):
        for k in range(src.shape[0]):
            step = src.shape[2] // parts
            for r in range(parts):
                at = pl.ds(r * step, step)
                move(src.at[k, 0, at], dst.at[k, 0, at])
    step = width // parts
    for r in range(parts):
        def write(i, carry):
            at = pl.ds(pl.multiple_of(r * step + i * tile, tile), tile)
            for c in range(cuts):
                orow[at, pl.ds(c * rows, rows)] = (dsum[c, at, :] + last[c, at, :].astype(F32)).astype(BF16)
            return carry

        lax.fori_loop(0, step // tile, write, 0)
        at = pl.ds(r * step, step)
        move(orow.at[at], orow_hbm.at[0, at])
    for done in moves:
        done.wait()


def written(gi, go, dsum, last):
    cuts, width, rows = dsum.shape
    shape = (1, width, cuts * rows)
    return pl.pallas_call(
        store,
        out_shape=tuple(jax.ShapeDtypeStruct(t, BF16) for t in (shape, gi.shape, go.shape)),
        in_specs=[pl.BlockSpec(memory_space=pltpu.VMEM)] * 4,
        out_specs=[pl.BlockSpec(memory_space=pl.ANY)] * 3,
        scratch_shapes=[pltpu.VMEM(shape[1:], BF16), pltpu.SemaphoreType.DMA((4 + 8 * gi.shape[0],))],
        compiler_params=pltpu.CompilerParams(vmem_limit_bytes=2 * 1024 * 1024),
    )(gi, go, dsum, last)


def per_device(n_tok, n_dp, row_input, out_grad, in_weight, out_weight):
    blocks, _, width, hid = in_weight.shape
    row_count = row_input.shape[2]
    cuts = max(1, row_count // 256)
    rows = row_count // cuts
    half = width // n_dp
    wide = (cuts, width, rows)
    deep = (cuts, hid, rows)
    vm = pltpu.VMEM
    dma = pltpu.SemaphoreType.DMA
    return written(*pl.pallas_call(
        functools.partial(kernel, n_tok, n_dp, cuts, 64, 256, width),
        out_shape=(
            pltpu.VMEM((blocks, 1, half, hid), BF16),
            pltpu.VMEM((blocks, 1, hid, half), BF16),
            pltpu.VMEM(wide, F32),
            pltpu.VMEM(wide, BF16),
        ),
        in_specs=[pl.BlockSpec(memory_space=pl.ANY)] * 4,
        out_specs=[pl.BlockSpec(memory_space=pltpu.VMEM)] * 4,
        scratch_shapes=[
            vm(wide, BF16),
            vm((blocks,) + wide, BF16),
            vm((2 * blocks - 1,) + wide, BF16),
            vm(wide, BF16),
            vm((blocks, width, hid), BF16),
            vm((blocks, hid, width), BF16),
            vm((blocks, hid, width), BF16),
            vm((blocks, width, hid), BF16),
            vm((blocks,) + wide, BF16),
            vm((blocks,) + deep, BF16),
            vm((blocks,) + deep, F32),
            vm((blocks,) + wide, BF16),
            vm((blocks,) + deep, BF16),
            vm((blocks,) + wide, BF16),
            vm((blocks,) + wide, BF16),
            vm((blocks,) + wide, BF16),
            vm((blocks,) + deep, BF16),
            vm(deep, BF16),
            vm((width, rows), F32),
            vm((blocks, cuts, 1, rows), F32),
            vm((blocks, cuts, 1, rows), F32),
            vm((1, rows), F32),
            dma((2 * cuts + 2 * blocks,)),
            dma((2 * blocks, cuts)),
            dma((2 * blocks, cuts)),
            dma((3, blocks, cuts)),
            dma((3, blocks, cuts)),
            dma((blocks, cuts)),
            dma((blocks, cuts)),
            pltpu.SemaphoreType.REGULAR,
        ],
        compiler_params=pltpu.CompilerParams(
            collective_id=0, has_side_effects=True, vmem_limit_bytes=54 * 1024 * 1024
        ),
    )(row_input, out_grad, in_weight, out_weight))


def solution(mesh):
    return jax.shard_map(
        functools.partial(per_device, mesh.shape["tok"], mesh.shape["dp"]),
        mesh=mesh,
        in_specs=(
            P("tok", None, "dp"),
            P("tok", None, "dp"),
            P(None, "tok", None, None),
            P(None, "tok", None, None),
        ),
        out_specs=(P("tok", None, "dp"), P(None, "tok", "dp", None), P(None, "tok", None, "dp")),
        check_vma=False,
    )
```

```python
import functools

import jax
import jax.numpy as jnp
from jax import lax
from jax.experimental import pallas as pl
from jax.experimental.pallas import tpu as pltpu
from jax.sharding import PartitionSpec as P

epsilon = 1e-05
MESH = pl.DeviceIdType.MESH
F32 = jnp.float32
BF16 = jnp.bfloat16


def gelu_parts(hidden):
    cumulative = 0.5 * (1.0 + lax.erf(hidden * 0.7071067811865476))
    density = jnp.exp(-0.5 * hidden * hidden) * 0.3989422804014327
    return (hidden * cumulative, cumulative + hidden * density)


def kernel(
    n_tok, n_dp, cuts, tile, span, piece,
    x_hbm, g_hbm, wi_hbm, wo_hbm,
    gi_s, go_s, dsum, last,
    x_in, x_hat, recv, grad, wi, wo, wit, wot, normed, act, deriv, dsl, dhid, low,
    normed_p, dsl_p, deriv_p, dhid_p, tmp, inv1, inv2, inv_p,
    ld_sem, z_send, z_recv, x_send, x_recv, p_send, p_recv,
):
    blocks, width, hid = wi.shape
    rows = x_in.shape[2]
    head = width // n_tok
    half = width // n_dp
    me = lax.axis_index("tok")
    mine = lax.axis_index("dp")
    other = lax.rem(mine + 1, n_dp)

    barrier = pltpu.get_barrier_semaphore()

    def greet(i, carry):
        peer = lax.rem(me + 1 + i, n_tok)
        pl.semaphore_signal(barrier, inc=1, device_id={"tok": peer}, device_id_type=MESH)
        return carry

    lax.fori_loop(0, n_tok - 1, greet, 0)
    pl.semaphore_signal(barrier, inc=1, device_id={"dp": other}, device_id_type=MESH)

    loads = []
    for c in range(cuts):
        loads.append(pltpu.make_async_copy(x_hbm.at[0, :, pl.ds(c * rows, rows)], x_in.at[c], ld_sem.at[c]))
    for c in range(cuts):
        loads.append(pltpu.make_async_copy(g_hbm.at[0, :, pl.ds(c * rows, rows)], grad.at[c], ld_sem.at[cuts + c]))
    for k in range(blocks):
        loads.append(pltpu.make_async_copy(wi_hbm.at[k, 0], wi.at[k], ld_sem.at[2 * cuts + 2 * k]))
        loads.append(pltpu.make_async_copy(wo_hbm.at[k, 0], wo.at[k], ld_sem.at[2 * cuts + 2 * k + 1]))
    for load in loads:
        load.start()

    pl.semaphore_wait(barrier, n_tok)

    team = n_tok // 2
    base = (me // team) * team
    lower = base == 0
    outer_half = jnp.where(lower, me, n_tok - 1 - me) < team // 2

    def spot(i):
        if team % 4:
            return i
        return i - lax.rem(i, 4) + 2 * lax.rem(i, 2) + lax.div(lax.rem(i, 4), 2)

    def land(m):
        return last if m == 2 * blocks - 1 else recv.at[m]

    def mix_send(src, m, c):
        def go(peer):
            pltpu.make_async_remote_copy(
                src_ref=src.at[pl.ds(pl.multiple_of(peer * head, head), head)],
                dst_ref=land(m).at[c, pl.ds(pl.multiple_of(me * head, head), head)],
                send_sem=z_send.at[m, c],
                recv_sem=z_recv.at[m, c],
                device_id={"tok": peer},
                device_id_type=MESH,
            ).start()

        def cross(i, carry):
            at = spot(i)
            go(jnp.where(lower, n_tok - 1 - at, at))
            return carry

        def local(i, carry):
            at = spot(lax.rem(i + team // 2, team))
            peer = jnp.where(lower, at, n_tok - 1 - at)
            pl.when(peer != me)(functools.partial(go, peer))
            return carry

        @pl.when(outer_half)
        def _():
            lax.fori_loop(0, team, lambda i, carry: local(i, cross(i, carry)), 0)

        @pl.when(jnp.logical_not(outer_half))
        def _():
            lax.fori_loop(0, team, cross, 0)
            lax.fori_loop(0, team, local, 0)

        own = pl.ds(pl.multiple_of(me * head, head), head)
        land(m)[c, own, :] = src[own, :]

    def mix_all(m, c):
        part = land(m).at[c, pl.ds(0, head * (n_tok - 1))]
        return pltpu.make_async_remote_copy(
            src_ref=part, dst_ref=part, send_sem=z_send.at[m, c], recv_sem=z_recv.at[m, c],
            device_id={"tok": lax.rem(me + 1, n_tok)}, device_id_type=MESH,
        )

    far = pl.ds(pl.multiple_of((team - base) * head, head), team * head)

    def team_send(k, c):
        def one(i, carry):
            peer = base + lax.rem(me - base + 1 + i, team)
            pltpu.make_async_remote_copy(
                src_ref=dhid_p.at[c, pl.ds(pl.multiple_of(peer * head, head), head)],
                dst_ref=normed_p.at[k, c, pl.ds(pl.multiple_of(me * head, head), head)],
                send_sem=p_send.at[k, c],
                recv_sem=p_recv.at[k, c],
                device_id={"tok": peer},
                device_id_type=MESH,
            ).start()
            return carry

        lax.fori_loop(0, team - 1, one, 0)
        own = pl.ds(pl.multiple_of(me * head, head), head)
        normed_p[k, c, own, :] = dhid_p[c, own, :]

    def team_all(k, c):
        part = normed_p.at[k, c, pl.ds(0, head * (team - 1))]
        return pltpu.make_async_remote_copy(
            src_ref=part, dst_ref=part, send_sem=p_send.at[k, c], recv_sem=p_recv.at[k, c],
            device_id={"tok": lax.rem(me + 1, n_tok)}, device_id_type=MESH,
        )

    def pair_part(kind, k, c, at):
        if kind == 0:
            src, dst = normed.at[k, c], normed_p.at[k, c]
        elif kind == 2:
            src, dst = recv.at[k, c], normed_p.at[k, c]
        else:
            src, dst = grad.at[c] if k == blocks - 1 else dsl.at[k, c], dsl_p.at[k, c]
        return pltpu.make_async_remote_copy(
            src_ref=src.at[at], dst_ref=dst.at[at],
            send_sem=x_send.at[kind, k, c], recv_sem=x_recv.at[kind, k, c],
            device_id={"dp": other}, device_id_type=MESH,
        )

    def pair(kind, k, c):
        return pair_part(kind, k, c, far if kind == 2 else pl.ds(0, width))

    def pair_send(kind, k, c):
        def one(i, carry):
            pair_part(kind, k, c, pl.ds(pl.multiple_of(i * piece, piece), piece)).start()
            return carry

        lax.fori_loop(0, width // piece, one, 0)

    def tiles(body, carry=0):
        def step(i, state):
            return body(pl.ds(pl.multiple_of(i * tile, tile), tile), state)

        return lax.fori_loop(0, width // tile, step, carry)

    zero = jnp.zeros((8, rows), F32)

    def fold(value):
        return jnp.sum(value.reshape(tile // 8, 8, rows), axis=0)

    def mean(total):
        return jnp.sum(total, axis=0, keepdims=True) * (1.0 / width)

    stride = min(2 * span, width)

    def matmul(left, right, sink):
        def step(i, carry):
            at = pl.ds(pl.multiple_of(i * stride, stride), stride)
            sink(at, jnp.dot(left[at, :], right[...], preferred_element_type=F32))
            return carry

        lax.fori_loop(0, left.shape[0] // stride, step, 0)

    def to_tmp(at, value):
        tmp[at, :] = value

    def norm_tmp(total, inv_ref, out_ref):
        center = mean(total)

        def spread(at, state):
            gap = tmp[at, :] - center
            return state + fold(gap * gap)

        inverse = lax.rsqrt(mean(tiles(spread, zero)) + epsilon)
        inv_ref[...] = inverse

        def write(at, state):
            out_ref[at, :] = ((tmp[at, :] - center) * inverse).astype(BF16)
            return state

        tiles(write)

    def forward(k, c):
        current = x_in.at[c] if k == 0 else x_hat.at[k - 1, c]

        def add(at, state):
            value = recv[k, c, at, :].astype(F32) + current[at, :].astype(F32)
            tmp[at, :] = value
            return state + fold(value)

        norm_tmp(tiles(add, zero), inv1.at[k, c], normed.at[k, c])
        if k == 0:
            pair_send(0, k, c)
        matmul(wit.at[k], normed.at[k, c], to_tmp)

        def gelu(at, state):
            first, second = gelu_parts(tmp[at, :])
            act[k, c, at, :] = first.astype(BF16)
            deriv[k, c, at, :] = second
            return state

        tiles(gelu)
        matmul(wot.at[k], act.at[k, c], to_tmp)

        def skip(at, state):
            value = tmp[at, :] + normed[k, c, at, :].astype(F32)
            tmp[at, :] = value
            return state + fold(value)

        norm_tmp(tiles(skip, zero), inv2.at[k, c], x_hat.at[k, c])

    def norm_back(means, hat, inverse, sink):
        up, cross = mean(means[0]), mean(means[1])

        def write(at, state):
            value = inverse * (tmp[at, :] - up - hat[at, :].astype(F32) * cross)
            sink(at, value)
            return state

        tiles(write)

    def backward(k, c):
        def upward(at, state):
            if k == blocks - 1:
                value = grad[c, at, :].astype(F32)
            else:
                value = dsum[c, at, :] + recv[2 * blocks - 2 - k, c, at, :].astype(F32)
                value = value.astype(BF16).astype(F32)
            tmp[at, :] = value
            return state[0] + fold(value), state[1] + fold(value * x_hat[k, c, at, :].astype(F32))

        def keep_second(at, value):
            tmp[at, :] = value
            dsl[k, c, at, :] = value.astype(BF16)

        norm_back(tiles(upward, (zero, zero)), x_hat.at[k, c], inv2[k, c], keep_second)
        if k < blocks - 1:
            pair_send(1, k, c)

        def hidden_sink(at, value):
            dhid[k, c, at, :] = (value * deriv[k, c, at, :]).astype(BF16)

        matmul(wo.at[k], dsl.at[k, c], hidden_sink)

        def add_tmp(at, value):
            tmp[at, :] = tmp[at, :] + value

        matmul(wi.at[k], dhid.at[k, c], add_tmp)

        def sums(at, state):
            value = tmp[at, :]
            return state[0] + fold(value), state[1] + fold(value * normed[k, c, at, :].astype(F32))

        def keep_summed(at, value):
            dsum[c, at, :] = value
            low[k, c, at, :] = value.astype(BF16)

        norm_back(tiles(sums, (zero, zero)), normed.at[k, c], inv1[k, c], keep_summed)
        mix_send(low.at[k, c], 2 * blocks - 1 - k, c)

    def peer_forward(k, c):
        if k == 0:
            pair(0, k, c).wait_recv()
        else:
            team_all(k, c).wait()
            pair(2, k, c).wait()

            def add(at, state):
                value = normed_p[k, c, at, :].astype(F32) + dhid_p[c, at, :].astype(F32)
                tmp[at, :] = value
                return state + fold(value)

            norm_tmp(tiles(add, zero), inv_p, normed_p.at[k, c])
        matmul(wit.at[k], normed_p.at[k, c], to_tmp)

        def gelu(at, state):
            first, second = gelu_parts(tmp[at, :])
            recv[k, c, at, :] = first.astype(BF16)
            deriv_p[k, c, at, :] = second.astype(BF16)
            return state

        tiles(gelu)
        matmul(wot.at[k], recv.at[k, c], to_tmp)

        def skip(at, state):
            value = tmp[at, :] + normed_p[k, c, at, :].astype(F32)
            tmp[at, :] = value
            return state + fold(value)

        norm_tmp(tiles(skip, zero), inv_p, dhid_p.at[c])
        if k < blocks - 1:
            team_send(k + 1, c)
            return
        pair(1, k, c).wait_recv()

        def upward(at, state):
            value = dsl_p[k, c, at, :].astype(F32)
            tmp[at, :] = value
            return state[0] + fold(value), state[1] + fold(value * dhid_p[c, at, :].astype(F32))

        def keep(at, value):
            dsl_p[k, c, at, :] = value.astype(BF16)

        norm_back(tiles(upward, (zero, zero)), dhid_p.at[c], inv_p[...], keep)

    def peer_backward(k, c):
        if k < blocks - 1:
            pair(1, k, c).wait_recv()

        def sink(at, value):
            dhid_p[c, at, :] = (value * deriv_p[k, c, at, :].astype(F32)).astype(BF16)

        matmul(wo.at[k], dsl_p.at[k, c], sink)

    def outer(left, right):
        return lax.dot_general(left, right, (((1,), (1,)), ((), ())), preferred_element_type=F32)

    part = pl.ds(pl.multiple_of(mine * half, half), half)

    wide_span = min(2 * span, half, hid)

    def bands(size, body):
        def step(i, carry):
            body(i * wide_span)
            return carry

        lax.fori_loop(0, size // wide_span, step, 0)

    def band(start):
        return pl.ds(pl.multiple_of(start, wide_span), wide_span)

    def own_grads(k):
        def first(start):
            src = band(mine * half + start)
            total = sum(outer(normed[k, c, src, :], dhid[k, c]) for c in range(cuts))
            gi_s[k, 0, band(start), :] = total.astype(BF16)

        bands(half, first)

        def second(start):
            at = band(start)
            total = sum(outer(act[k, c, at, :], dsl[k, c, part, :]) for c in range(cuts))
            go_s[k, 0, at, :] = total.astype(BF16)

        bands(hid, second)

    def peer_grads(k):
        def put(out, at, total):
            out[k, 0, at, :] = (out[k, 0, at, :].astype(F32) + total.astype(BF16).astype(F32)).astype(BF16)

        def first(start):
            src = band(mine * half + start)
            put(gi_s, band(start), sum(outer(normed_p[k, c, src, :], dhid_p[c]) for c in range(cuts)))

        bands(half, first)

        def second(start):
            at = band(start)
            put(go_s, at, sum(outer(recv[k, c, at, :], dsl_p[k, c, part, :]) for c in range(cuts)))

        bands(hid, second)

    def each(body):
        def step(c, carry):
            body(c)
            return carry

        lax.fori_loop(0, cuts, step, 0)

    for c in range(cuts):
        loads[c].wait()
        mix_send(x_in.at[c], 0, c)
    for c in range(cuts):
        loads[cuts + c].wait()
    pair_send(1, blocks - 1, 0)
    for load in loads[2 * cuts:]:
        load.wait()
    edge = min(256, width, hid)

    def flip(i, carry):
        a = pl.ds(pl.multiple_of(lax.rem(i, hid // edge) * edge, edge), edge)
        for k in range(blocks):
            for j in range(width // edge):
                b = pl.ds(j * edge, edge)
                wit[k, a, b] = wi[k, b, a].T
                wot[k, b, a] = wo[k, a, b].T
        return carry

    lax.fori_loop(0, hid // edge, flip, 0)

    def ahead(k, c):
        if k > 0:
            peer_forward(k - 1, c)
        mix_all(k, c).wait_recv()
        if k > 0:
            pair_part(2, k, c, far).start()
        forward(k, c)
        if k < blocks - 1:
            mix_send(x_hat.at[k, c], k + 1, c)
        else:
            backward(k, c)

    def last_ahead(c):
        peer_forward(blocks - 1, c)
        peer_backward(blocks - 1, c)
        mix_all(blocks, c).wait_recv()
        backward(blocks - 2, c)

    each(functools.partial(ahead, 0))
    for c in range(1, cuts):
        pair_send(1, blocks - 1, c)
    for k in range(1, blocks):
        each(functools.partial(ahead, k))
    own_grads(blocks - 1)
    each(last_ahead)
    peer_grads(blocks - 1)
    for k in reversed(range(blocks - 1)):
        peer_backward(k, 0)
        own_grads(k)
        for c in range(1, cuts):
            peer_backward(k, c)
        peer_grads(k)
    for c in range(cuts):
        mix_all(2 * blocks - 1, c).wait_recv()
        pair(0, 0, c).wait_send()
        for k in range(blocks):
            pair(1, k, c).wait_send()
        for m in range(2 * blocks):
            mix_all(m, c).wait_send()


def store(gi, go, dsum, last, orow_hbm, gi_hbm, go_hbm, orow, sem):
    cuts, width, rows = dsum.shape
    tile, parts = 64, 4
    moves = []

    def move(src, dst):
        moves.append(pltpu.make_async_copy(src, dst, sem.at[len(moves)]))
        moves[-1].start()

    for src, dst in ((gi, gi_hbm), (go, go_hbm)):
        for k in range(src.shape[0]):
            step = src.shape[2] // parts
            for r in range(parts):
                at = pl.ds(r * step, step)
                move(src.at[k, 0, at], dst.at[k, 0, at])
    step = width // parts
    for r in range(parts):
        def write(i, carry):
            at = pl.ds(pl.multiple_of(r * step + i * tile, tile), tile)
            for c in range(cuts):
                orow[at, pl.ds(c * rows, rows)] = (dsum[c, at, :] + last[c, at, :].astype(F32)).astype(BF16)
            return carry

        lax.fori_loop(0, step // tile, write, 0)
        at = pl.ds(r * step, step)
        move(orow.at[at], orow_hbm.at[0, at])
    for done in moves:
        done.wait()


def written(gi, go, dsum, last):
    cuts, width, rows = dsum.shape
    shape = (1, width, cuts * rows)
    return pl.pallas_call(
        store,
        out_shape=tuple(jax.ShapeDtypeStruct(t, BF16) for t in (shape, gi.shape, go.shape)),
        in_specs=[pl.BlockSpec(memory_space=pltpu.VMEM)] * 4,
        out_specs=[pl.BlockSpec(memory_space=pl.ANY)] * 3,
        scratch_shapes=[pltpu.VMEM(shape[1:], BF16), pltpu.SemaphoreType.DMA((4 + 8 * gi.shape[0],))],
        compiler_params=pltpu.CompilerParams(vmem_limit_bytes=2 * 1024 * 1024),
    )(gi, go, dsum, last)


def per_device(n_tok, n_dp, row_input, out_grad, in_weight, out_weight):
    blocks, _, width, hid = in_weight.shape
    row_count = row_input.shape[2]
    cuts = max(1, row_count // 256)
    rows = row_count // cuts
    half = width // n_dp
    wide = (cuts, width, rows)
    deep = (cuts, hid, rows)
    vm = pltpu.VMEM
    dma = pltpu.SemaphoreType.DMA
    return written(*pl.pallas_call(
        functools.partial(kernel, n_tok, n_dp, cuts, 64, 256, width),
        out_shape=(
            pltpu.VMEM((blocks, 1, half, hid), BF16),
            pltpu.VMEM((blocks, 1, hid, half), BF16),
            pltpu.VMEM(wide, F32),
            pltpu.VMEM(wide, BF16),
        ),
        in_specs=[pl.BlockSpec(memory_space=pl.ANY)] * 4,
        out_specs=[pl.BlockSpec(memory_space=pltpu.VMEM)] * 4,
        scratch_shapes=[
            vm(wide, BF16),
            vm((blocks,) + wide, BF16),
            vm((2 * blocks - 1,) + wide, BF16),
            vm(wide, BF16),
            vm((blocks, width, hid), BF16),
            vm((blocks, hid, width), BF16),
            vm((blocks, hid, width), BF16),
            vm((blocks, width, hid), BF16),
            vm((blocks,) + wide, BF16),
            vm((blocks,) + deep, BF16),
            vm((blocks,) + deep, F32),
            vm((blocks,) + wide, BF16),
            vm((blocks,) + deep, BF16),
            vm((blocks,) + wide, BF16),
            vm((blocks,) + wide, BF16),
            vm((blocks,) + wide, BF16),
            vm((blocks,) + deep, BF16),
            vm(deep, BF16),
            vm((width, rows), F32),
            vm((blocks, cuts, 1, rows), F32),
            vm((blocks, cuts, 1, rows), F32),
            vm((1, rows), F32),
            dma((2 * cuts + 2 * blocks,)),
            dma((2 * blocks, cuts)),
            dma((2 * blocks, cuts)),
            dma((3, blocks, cuts)),
            dma((3, blocks, cuts)),
            dma((blocks, cuts)),
            dma((blocks, cuts)),
        ],
        compiler_params=pltpu.CompilerParams(
            collective_id=0, has_side_effects=True, vmem_limit_bytes=54 * 1024 * 1024
        ),
    )(row_input, out_grad, in_weight, out_weight))


def solution(mesh):
    return jax.shard_map(
        functools.partial(per_device, mesh.shape["tok"], mesh.shape["dp"]),
        mesh=mesh,
        in_specs=(
            P("tok", None, "dp"),
            P("tok", None, "dp"),
            P(None, "tok", None, None),
            P(None, "tok", None, None),
        ),
        out_specs=(P("tok", None, "dp"), P(None, "tok", "dp", None), P(None, "tok", None, "dp")),
        check_vma=False,
    )
```
